128 devices in a mesh: light: 8 (over z, core), view: 16 (over x, y).
Axes of the slice: x: 4, y: 4, z: 4, core: 2. Of those that a mesh axis runs over, the one named last changes fastest.
Arguments:
- density: bfloat16 [2048, 64, 1024], P('view', None, 'light'), may hold values from 0 to 8, as said below
- color_coef: float32 [3, 4], replicated, may hold values from 0.2 to 1
Outputs:
- image: float32 [3, 64, 1024], P(None, 'view', 'light')
The draws below stay inside these ranges and needn't reach their ends.
Inputs may be any that keep to these rules, and one draw needn't show every extreme that they name: `density`: densities are nonnegative.
All inputs are finite; a program needn't handle non-finite values.
Results may differ from the reference program's by a relative error of at most 0.0003.
Values sent between devices are 32-bit elements; how exact they have to be, the bound alone decides.
A program may use at most 64 MiB of HBM per device.

```python
import math
import jax
import jax.numpy as jnp
from jax import lax

CV = 128
CL = 128
Z = 64
NV = 2048
NL = 1024


def draw_density(key, part):
    view_tile = max(CV // 2, 1)
    key_rough, key_level = jax.random.split(key, 2)
    rough_part = jax.random.uniform(key_rough, (NV, Z, NL), jnp.float32, 0.0, 1.0)
    level_grid = jnp.exp(jax.random.uniform(key_level, (NV // view_tile, Z, NL // CL), jnp.float32, math.log(0.25), math.log(4.0)))
    level_grid = jnp.repeat(jnp.repeat(level_grid, view_tile, axis=0), CL, axis=2)
    return (rough_part * level_grid).astype(jnp.bfloat16)


def setup_inputs(seed: int = 0) -> dict:
    streams_of = jax.random.split(jax.random.key(seed), 3)
    density = draw_density(jax.random.fold_in(streams_of[2], 71), 0)
    color_coef = jnp.clip(jax.random.uniform(streams_of[1], (3, 4), jnp.float32, 0.2, 1.0), 0.2, 1.0)
    return {"density": density, "color_coef": color_coef}


def reference(density, color_coef):
    total_view = density.shape[0]
    block_rows = math.gcd(total_view, 128)
    blocks = density.reshape(total_view // block_rows, block_rows, Z, NL)

    def advance(carry, block):
        depth_sheet, picture = carry
        values = block.astype(jnp.float32)
        light_step = (2.0 / NL) * values
        lit = jnp.exp(-(jnp.cumsum(light_step, axis=2) - light_step))
        view_step = (2.0 / NV) * values
        view_depth = depth_sheet[None] + jnp.cumsum(view_step, axis=0) - view_step
        alpha = 1.0 - jnp.exp(-view_step)
        weight = alpha * (0.3 + lit) * jnp.exp(-view_depth)
        coef = color_coef[:, :, None, None, None]
        palette = coef[:, 0] + values[None] * (coef[:, 1] + values[None] * (coef[:, 2] + values[None] * coef[:, 3]))
        picture = picture + jnp.sum(palette * weight[None], axis=1)
        depth_sheet = depth_sheet + jnp.sum(view_step, axis=0)
        return (depth_sheet, picture), None

    start = (jnp.zeros((Z, NL), jnp.float32), jnp.zeros((3, Z, NL), jnp.float32))
    (depth_sheet, picture), unused = lax.scan(advance, start, blocks)
    return picture
```

```python
import functools
import math

import jax
import jax.numpy as jnp
from jax import lax
from jax.experimental import pallas as pl
from jax.experimental.pallas import tpu as pltpu
from jax.sharding import PartitionSpec as P

F32 = jnp.float32
BF16 = jnp.bfloat16
LOG2E = math.log2(math.e)
ROWS = 16
BLOCK = 16
TURN = (2, 1, 3, 0)


def kernel(
    light_total, view_total, light_count, view_count, far,
    x_hbm, coef_hbm, out_ref,
    xv, coef_s, own_sum, sib_sum, chip_sum, low_sum, upper, lit_alpha, base, piece, got,
    x_sem, coef_sem, sib_send, sib_recv, low_send, low_recv, piece_send, piece_recv,
):
    li = lax.axis_index("light")
    vi = lax.axis_index("view")
    chip, core = li // 2, li % 2
    chips = light_count // 2
    cells = x_hbm.shape[0]
    lanes = x_hbm.shape[2]
    planes = x_hbm.shape[1]
    chunks = planes // ROWS
    rows = planes // view_count
    per_chunk = ROWS // rows
    vx = vi // per_chunk

    def load(k):
        z0 = pl.multiple_of(((vx + TURN[k]) % chunks) * ROWS, ROWS)
        return pltpu.make_async_copy(x_hbm.at[:, pl.ds(z0, ROWS), :], xv.at[k], x_sem.at[k])

    def sib_copy(k):
        return pltpu.make_async_remote_copy(
            src_ref=own_sum.at[k], dst_ref=sib_sum.at[k], send_sem=sib_send.at[k], recv_sem=sib_recv.at[k],
            device_id=(chip * 2 + 1, vi), device_id_type=pl.DeviceIdType.MESH)

    def low_copy(k, to_chip, to_core):
        return pltpu.make_async_remote_copy(
            src_ref=chip_sum.at[k], dst_ref=low_sum.at[chip, k],
            send_sem=low_send.at[to_chip - 1, to_core, k], recv_sem=low_recv.at[chip, k],
            device_id=(to_chip * 2 + to_core, vi), device_id_type=pl.DeviceIdType.MESH)

    def low_arrival(k, from_chip):
        return pltpu.make_async_remote_copy(
            src_ref=chip_sum.at[k], dst_ref=low_sum.at[from_chip, k],
            send_sem=low_send.at[0, 0, k], recv_sem=low_recv.at[from_chip, k],
            device_id=(from_chip * 2 + 1, vi), device_id_type=pl.DeviceIdType.MESH)

    def piece_copy(k, d, j):
        return pltpu.make_async_remote_copy(
            src_ref=piece.at[k, d], dst_ref=got.at[vi], send_sem=piece_send.at[k, d], recv_sem=piece_recv.at[vi],
            device_id=(li, j), device_id_type=pl.DeviceIdType.MESH)

    def piece_arrival(i):
        return pltpu.make_async_remote_copy(
            src_ref=piece.at[0, 0], dst_ref=got.at[i], send_sem=piece_send.at[0, 0], recv_sem=piece_recv.at[i],
            device_id=(li, (vi + 1) % view_count), device_id_type=pl.DeviceIdType.MESH)

    for k in range(chunks):
        load(k).start()
    coef_copy = pltpu.make_async_copy(coef_hbm, coef_s, coef_sem)
    coef_copy.start()

    barrier = pltpu.get_barrier_semaphore()
    for other in range(1, view_count):
        pl.semaphore_signal(barrier, inc=1, device_id=(li, (vi + other) % view_count), device_id_type=pl.DeviceIdType.MESH)

    @pl.when(core == 1)
    def _():
        pl.semaphore_signal(barrier, inc=1, device_id=(li - 1, vi), device_id_type=pl.DeviceIdType.MESH)

    for c in range(chips - 1):
        @pl.when(c < chip)
        def _():
            pl.semaphore_signal(barrier, inc=1, device_id=(2 * c + 1, vi), device_id_type=pl.DeviceIdType.MESH)

    lane = lax.broadcasted_iota(jnp.int32, (ROWS, lanes), 1)
    r = lax.broadcasted_iota(jnp.int32, (lanes, lanes), 0)
    c = lax.broadcasted_iota(jnp.int32, (lanes, lanes), 1)
    before = jnp.where(r < c, 1.0, 0.0).astype(BF16)
    ones = jnp.ones((lanes, lanes), BF16)

    def block_of(k, b):
        return xv[k, pl.ds(b * BLOCK, BLOCK)].reshape(BLOCK * ROWS, lanes)

    for k in range(chunks):
        load(k).wait()

        def gather(b, acc):
            total = jnp.dot(block_of(k, b), ones, preferred_element_type=F32).reshape(BLOCK, ROWS, lanes)
            for v in range(BLOCK):
                acc = jnp.where(lane == b * BLOCK + v, total[v], acc)
            return acc

        own_sum[k] = lax.fori_loop(0, cells // BLOCK, gather, jnp.zeros((ROWS, lanes), F32))
        if k == 0:
            pl.semaphore_wait(barrier, (view_count - 1) + jnp.where(core == 0, 1, 2 * (chips - 1 - chip)))

        @pl.when(core == 0)
        def _():
            sib_copy(k).start()

    @pl.when(core == 1)
    def _():
        for k in range(chunks):
            sib_copy(k).wait_recv()
            chip_sum[k] = own_sum[k] + sib_sum[k]
            for to_chip in range(1, chips):
                @pl.when(to_chip > chip)
                def _():
                    for to_core in range(2):
                        low_copy(k, to_chip, to_core).start()

    view_scale = -LOG2E * 2.0 / view_total
    light_scale = -LOG2E * 2.0 / light_total
    for k in range(chunks):
        def local(b, carry):
            clear, m0, m1, m2, m3 = carry
            xb = block_of(k, b)
            depth = jnp.dot(xb, before, preferred_element_type=F32).reshape(BLOCK, ROWS, lanes)
            xb = xb.reshape(BLOCK, ROWS, lanes)
            for v in range(BLOCK):
                x = xb[v].astype(F32)
                beyond = clear * jnp.exp2(view_scale * x)
                a = clear - beyond
                clear = beyond
                lit_alpha[k, b * BLOCK + v] = a * jnp.exp2(light_scale * depth[v])
                m0 = m0 + a
                a = a * x
                m1 = m1 + a
                a = a * x
                m2 = m2 + a
                a = a * x
                m3 = m3 + a
            return clear, m0, m1, m2, m3

        zero = jnp.zeros((ROWS, lanes), F32)
        clear, *sums = lax.fori_loop(0, cells // BLOCK, local, (jnp.ones((ROWS, lanes), F32), zero, zero, zero, zero))
        base[k, 4] = clear
        for i in range(4):
            base[k, i] = 0.3 * sums[i]

    coef_copy.wait()
    for k in range(chunks):
        upper[...] = jnp.zeros_like(upper)

        @pl.when(core == 1)
        def _():
            upper[...] += sib_sum[k]

        for c in range(chips - 1):
            @pl.when(c < chip)
            def _():
                low_arrival(k, c).wait_recv()
                upper[...] += low_sum[c, k]

        dim = jnp.exp2(light_scale * upper[...])

        def lighted(b, carry):
            m0, m1, m2, m3 = carry
            near = pltpu.roll(dim, (lanes - b * BLOCK) % lanes, 1)
            xb = xv[k, pl.ds(b * BLOCK, BLOCK)]
            for v in range(BLOCK):
                x = xb[v].astype(F32)
                a = lit_alpha[k, b * BLOCK + v] * jnp.broadcast_to(near[:, v : v + 1], (ROWS, lanes))
                m0 = m0 + a
                a = a * x
                m1 = m1 + a
                a = a * x
                m2 = m2 + a
                a = a * x
                m3 = m3 + a
            return m0, m1, m2, m3

        sums = lax.fori_loop(0, cells // BLOCK, lighted, tuple(base[k, i] for i in range(4)))
        parts = [
            coef_s[ch, 0] * sums[0] + coef_s[ch, 1] * sums[1] + coef_s[ch, 2] * sums[2] + coef_s[ch, 3] * sums[3]
            for ch in range(3)
        ] + [base[k, 4]]
        to = ((vx + TURN[k]) % chunks) * per_chunk
        for d in range(per_chunk):
            mine = jnp.concatenate([p[d * rows : (d + 1) * rows] for p in parts], axis=0)
            piece[k, d] = mine
            j = to + d

            @pl.when(j == vi)
            def _():
                got[vi] = mine

            @pl.when(j != vi)
            def _():
                piece_copy(k, d, j).start()

    for i in range(view_count):
        @pl.when(i != vi)
        def _():
            piece_arrival(i).wait_recv()

    clear = jnp.ones((rows, lanes), F32)
    total = [jnp.zeros((rows, lanes), F32) for _ in range(3)]
    for i in range(view_count):
        for ch in range(3):
            total[ch] = total[ch] + clear * got[i, ch * rows : (ch + 1) * rows]
        clear = clear * got[i, 3 * rows : 4 * rows]
    for ch in range(3):
        out_ref[ch] = total[ch]

    @pl.when(core == 0)
    def _():
        for k in range(chunks):
            sib_copy(k).wait_send()

    @pl.when(core == 1)
    def _():
        for k in range(chunks):
            for to_chip in range(1, chips):
                @pl.when(to_chip > chip)
                def _():
                    for to_core in range(2):
                        low_copy(k, to_chip, to_core).wait_send()

    for k in range(chunks):
        to = ((vx + TURN[k]) % chunks) * per_chunk
        for d in range(per_chunk):
            @pl.when(to + d != vi)
            def _():
                piece_copy(k, d, to + d).wait_send()


def body(density, color_coef):
    cells, planes, lanes = density.shape
    light_count = lax.axis_size("light")
    view_count = lax.axis_size("view")
    chips = light_count // 2
    chunks = planes // ROWS
    rows = planes // view_count
    per_chunk = ROWS // rows
    dma = pltpu.SemaphoreType.DMA
    return pl.pallas_call(
        functools.partial(kernel, lanes * light_count, cells * view_count, light_count, view_count, None),
        out_shape=jax.ShapeDtypeStruct((3, rows, lanes), F32),
        in_specs=[pl.BlockSpec(memory_space=pl.ANY), pl.BlockSpec(memory_space=pl.ANY)],
        out_specs=pl.BlockSpec(memory_space=pltpu.VMEM),
        scratch_shapes=[
            pltpu.VMEM((chunks, cells, ROWS, lanes), BF16),
            pltpu.SMEM((3, 4), F32),
            pltpu.VMEM((chunks, ROWS, lanes), F32),
            pltpu.VMEM((chunks, ROWS, lanes), F32),
            pltpu.VMEM((chunks, ROWS, lanes), F32),
            pltpu.VMEM((chips - 1, chunks, ROWS, lanes), F32),
            pltpu.VMEM((ROWS, lanes), F32),
            pltpu.VMEM((chunks, cells, ROWS, lanes), F32),
            pltpu.VMEM((chunks, 5, ROWS, lanes), F32),
            pltpu.VMEM((chunks, per_chunk, 4 * rows, lanes), F32),
            pltpu.VMEM((view_count, 4 * rows, lanes), F32),
            dma((chunks,)),
            dma,
            dma((chunks,)),
            dma((chunks,)),
            dma((chips - 1, 2, chunks)),
            dma((chips - 1, chunks)),
            dma((chunks, per_chunk)),
            dma((view_count,)),
        ],
        compiler_params=pltpu.CompilerParams(collective_id=0, has_side_effects=True),
    )(density, color_coef)


def solution(mesh):
    placed = (P("view", None, "light"), P())
    return jax.shard_map(
        body, mesh=mesh, in_specs=placed, out_specs=P(None, "view", "light"), check_vma=False
    )
```

```python
import functools
import math

import jax
import jax.numpy as jnp
from jax import lax
from jax.experimental import pallas as pl
from jax.experimental.pallas import tpu as pltpu
from jax.sharding import PartitionSpec as P

F32 = jnp.float32
BF16 = jnp.bfloat16
LOG2E = math.log2(math.e)
ROWS = 16
BLOCK = 16
HALF = BLOCK // 2
TURN = (2, 1, 3, 0)
AMBIENT = 0.3
MESH = pl.DeviceIdType.MESH


def kernel(
    light_total, view_total, light_count, view_count,
    x_hbm, coef_hbm, out_ref,
    xv, coef_s, own_sum, sib_sum, chip_sum, low_sum, upper, dim_t, dims, xf, alpha, lit_alpha, clears, piece, got,
    x_sem, coef_sem, sib_send, sib_recv, low_send, low_recv, piece_send, piece_recv,
):
    li = lax.axis_index("light")
    vi = lax.axis_index("view")
    chip, core = li // 2, li % 2
    chips = light_count // 2
    cells, planes, lanes = x_hbm.shape
    chunks = planes // ROWS
    rows = planes // view_count
    per_chunk = ROWS // rows
    steps = cells // BLOCK
    vx = vi // per_chunk

    def load(k):
        z0 = pl.multiple_of(((vx + TURN[k]) % chunks) * ROWS, ROWS)
        return pltpu.make_async_copy(x_hbm.at[:, pl.ds(z0, ROWS), :], xv.at[k], x_sem.at[k])

    def sib_copy(k):
        return pltpu.make_async_remote_copy(
            src_ref=own_sum.at[k], dst_ref=sib_sum.at[k], send_sem=sib_send.at[k], recv_sem=sib_recv.at[k],
            device_id=(chip * 2 + 1, vi), device_id_type=MESH)

    def low_copy(k, to_chip, to_core):
        return pltpu.make_async_remote_copy(
            src_ref=chip_sum.at[k], dst_ref=low_sum.at[chip, k],
            send_sem=low_send.at[to_chip - 1, to_core, k], recv_sem=low_recv.at[chip, k],
            device_id=(to_chip * 2 + to_core, vi), device_id_type=MESH)

    def low_arrival(k, from_chip):
        return pltpu.make_async_remote_copy(
            src_ref=chip_sum.at[k], dst_ref=low_sum.at[from_chip, k],
            send_sem=low_send.at[0, 0, k], recv_sem=low_recv.at[from_chip, k],
            device_id=(from_chip * 2 + 1, vi), device_id_type=MESH)

    def piece_copy(k, d, j):
        return pltpu.make_async_remote_copy(
            src_ref=piece.at[k, d], dst_ref=got.at[vi], send_sem=piece_send, recv_sem=piece_recv,
            device_id=(li, j), device_id_type=MESH)

    def all_pieces():
        others = pl.ds(0, view_count - 1)
        return pltpu.make_async_remote_copy(
            src_ref=got.at[others], dst_ref=got.at[others], send_sem=piece_send, recv_sem=piece_recv,
            device_id=(li, (vi + 1) % view_count), device_id_type=MESH)

    for k in range(chunks):
        load(k).start()
    coef_copy = pltpu.make_async_copy(coef_hbm, coef_s, coef_sem)
    coef_copy.start()

    barrier = pltpu.get_barrier_semaphore()

    @pl.when(core == 1)
    def _():
        pl.semaphore_signal(barrier, inc=1, device_id=(li - 1, vi), device_id_type=MESH)

    for c in range(chips - 1):
        @pl.when(c < chip)
        def _():
            pl.semaphore_signal(barrier, inc=1, device_id=(2 * c + 1, vi), device_id_type=MESH)

    for other in range(1, view_count):
        pl.semaphore_signal(barrier, inc=1, device_id=(li, (vi + other) % view_count), device_id_type=MESH)

    row = lax.broadcasted_iota(jnp.int32, (ROWS, lanes), 0)
    for k in range(chunks):
        load(k).wait()
        acc = jnp.zeros((steps, BLOCK * ROWS), F32)
        for p in range(steps):
            xb = xv[k, p * BLOCK : (p + 1) * BLOCK].reshape(BLOCK * ROWS, lanes)
            pick = jnp.where(row == p, 1.0, 0.0).astype(BF16)[:steps]
            acc = acc + lax.dot_general(pick, xb, (((1,), (1,)), ((), ())), preferred_element_type=F32)
        own_sum[k, 0:steps] = acc[:, : HALF * ROWS]
        own_sum[k, steps:] = acc[:, HALF * ROWS :]
        if k == 0:
            pl.semaphore_wait(barrier, (view_count - 1) + jnp.where(core == 0, 1, 2 * (chips - 1 - chip)))

        @pl.when(core == 0)
        def _():
            sib_copy(k).start()

    @pl.when(core == 1)
    def _():
        for k in range(chunks):
            sib_copy(k).wait_recv()
            chip_sum[k] = own_sum[k] + sib_sum[k]
            for to_chip in range(1, chips):
                @pl.when(to_chip > chip)
                def _():
                    for to_core in range(2):
                        low_copy(k, to_chip, to_core).start()

    view_scale = -LOG2E * 2.0 / view_total
    light_scale = -LOG2E * 2.0 / light_total
    r = lax.broadcasted_iota(jnp.int32, (lanes, lanes), 0)
    c = lax.broadcasted_iota(jnp.int32, (lanes, lanes), 1)
    before = jnp.where(r < c, 1.0, 0.0).astype(BF16)
    for k in range(chunks):
        def local(b, clear):
            xb = xv[k, pl.ds(b * BLOCK, BLOCK)].reshape(BLOCK * ROWS, lanes)
            depth = jnp.dot(xb, before, preferred_element_type=F32).reshape(BLOCK, ROWS, lanes)
            xb = xb.reshape(BLOCK, ROWS, lanes)
            for v in range(BLOCK):
                x = xb[v].astype(F32)
                beyond = clear * jnp.exp2(view_scale * x)
                a = clear - beyond
                clear = beyond
                xf[k, b * BLOCK + v] = x
                alpha[k, b * BLOCK + v] = a
                lit_alpha[k, b * BLOCK + v] = a * jnp.exp2(light_scale * depth[v])
            return clear

        clears[k] = lax.fori_loop(0, steps, local, jnp.ones((ROWS, lanes), F32))

    coef_copy.wait()
    for k in range(chunks):
        upper[...] = jnp.zeros_like(upper)

        @pl.when(core == 1)
        def _():
            upper[...] += sib_sum[k]

        for c in range(chips - 1):
            @pl.when(c < chip)
            def _():
                low_arrival(k, c).wait_recv()
                upper[...] += low_sum[c, k]

        dim_t[...] = jnp.transpose(jnp.exp2(light_scale * upper[...]) * (1.0 / AMBIENT))

        def spread(p):
            for h in range(2):
                at = jnp.full((HALF * ROWS, 2 * steps), h * steps, jnp.int32) + p
                near = jnp.take_along_axis(dim_t[...], jnp.broadcast_to(at[:, :1], (HALF * ROWS, lanes)), axis=1)
                dims[p % 2, h * HALF : (h + 1) * HALF] = near.reshape(HALF, ROWS, lanes)

        def lighted(p, carry):
            m0, m1, m2, m3 = carry
            spread(p)
            for v in range(BLOCK):
                x = xf[k, p * BLOCK + v]
                a = alpha[k, p * BLOCK + v] + lit_alpha[k, p * BLOCK + v] * dims[p % 2, v]
                m0 = m0 + a
                a = a * x
                m1 = m1 + a
                a = a * x
                m2 = m2 + a
                a = a * x
                m3 = m3 + a
            return m0, m1, m2, m3

        zero = jnp.zeros((ROWS, lanes), F32)
        sums = lax.fori_loop(0, steps, lighted, (zero, zero, zero, zero))
        parts = []
        for ch in range(3):
            t = coef_s[ch, 0] * sums[0] + coef_s[ch, 1] * sums[1] + coef_s[ch, 2] * sums[2] + coef_s[ch, 3] * sums[3]
            parts.append(AMBIENT * t)
        parts.append(clears[k])
        to = ((vx + TURN[k]) % chunks) * per_chunk
        for d in range(per_chunk):
            mine = jnp.concatenate([p[d * rows : (d + 1) * rows] for p in parts], axis=0)
            piece[k, d] = mine
            j = to + d

            @pl.when(j == vi)
            def _():
                got[vi] = mine

            @pl.when(j != vi)
            def _():
                piece_copy(k, d, j).start()

    all_pieces().wait_recv()
    half = lax.broadcasted_iota(jnp.int32, (2 * rows, lanes), 0)
    clear = jnp.ones((2 * rows, lanes), F32)
    total = [jnp.zeros((2 * rows, lanes), F32) for _ in range(2)]
    for i in range(view_count):
        first, second = got[i, : 2 * rows], got[i, 2 * rows :]
        total[0] = total[0] + clear * first
        total[1] = total[1] + clear * second
        clear = clear * jnp.where(half < rows, pltpu.roll(second, rows, 0), second)
    out_ref[0] = total[0][:rows]
    out_ref[1] = total[0][rows:]
    out_ref[2] = total[1][:rows]

    all_pieces().wait_send()

    @pl.when(core == 0)
    def _():
        for k in range(chunks):
            sib_copy(k).wait_send()

    @pl.when(core == 1)
    def _():
        for k in range(chunks):
            for to_chip in range(1, chips):
                @pl.when(to_chip > chip)
                def _():
                    for to_core in range(2):
                        low_copy(k, to_chip, to_core).wait_send()


def body(density, color_coef):
    cells, planes, lanes = density.shape
    light_count = lax.axis_size("light")
    view_count = lax.axis_size("view")
    chips = light_count // 2
    chunks = planes // ROWS
    rows = planes // view_count
    per_chunk = ROWS // rows
    dma = pltpu.SemaphoreType.DMA
    return pl.pallas_call(
        functools.partial(kernel, lanes * light_count, cells * view_count, light_count, view_count),
        out_shape=jax.ShapeDtypeStruct((3, rows, lanes), F32),
        in_specs=[pl.BlockSpec(memory_space=pl.ANY), pl.BlockSpec(memory_space=pl.ANY)],
        out_specs=pl.BlockSpec(memory_space=pltpu.VMEM),
        scratch_shapes=[
            pltpu.VMEM((chunks, cells, ROWS, lanes), BF16),
            pltpu.SMEM((3, 4), F32),
            pltpu.VMEM((chunks, ROWS, lanes), F32),
            pltpu.VMEM((chunks, ROWS, lanes), F32),
            pltpu.VMEM((chunks, ROWS, lanes), F32),
            pltpu.VMEM((chips - 1, chunks, ROWS, lanes), F32),
            pltpu.VMEM((ROWS, lanes), F32),
            pltpu.VMEM((HALF * ROWS, ROWS), F32),
            pltpu.VMEM((2, BLOCK, ROWS, lanes), F32),
            pltpu.VMEM((chunks, cells, ROWS, lanes), F32),
            pltpu.VMEM((chunks, cells, ROWS, lanes), F32),
            pltpu.VMEM((chunks, cells, ROWS, lanes), F32),
            pltpu.VMEM((chunks, ROWS, lanes), F32),
            pltpu.VMEM((chunks, per_chunk, 4 * rows, lanes), F32),
            pltpu.VMEM((view_count, 4 * rows, lanes), F32),
            dma((chunks,)),
            dma,
            dma((chunks,)),
            dma((chunks,)),
            dma((chips - 1, 2, chunks)),
            dma((chips - 1, chunks)),
            dma,
            dma,
        ],
        compiler_params=pltpu.CompilerParams(collective_id=0, has_side_effects=True),
    )(density, color_coef)


def solution(mesh):
    placed = (P("view", None, "light"), P())
    return jax.shard_map(
        body, mesh=mesh, in_specs=placed, out_specs=P(None, "view", "light"), check_vma=False
    )
```

```python
import functools
import math

import jax
import jax.numpy as jnp
from jax import lax
from jax.experimental import pallas as pl
from jax.experimental.pallas import tpu as pltpu
from jax.sharding import PartitionSpec as P

F32 = jnp.float32
BF16 = jnp.bfloat16
LOG2E = math.log2(math.e)
ROWS = 16
BLOCK = 16
HALF = BLOCK // 2
TURN = (2, 1, 3, 0)
AMBIENT = 0.3
ORDER = ("A0123", "M", "S0123", "L0", "C0123", "L12", "W", "B0", "L3", "B123")
MESH = pl.DeviceIdType.MESH


def kernel(
    light_total, view_total, light_count, view_count,
    x_hbm, coef_hbm, out_ref,
    xv, coef_s, own_sum, sib_sum, chip_sum, low_sum, upper, dim_t, dims, xf, alpha, lit_alpha, clears, piece, got,
    x_sem, coef_sem, sib_send, sib_recv, low_send, low_recv, piece_send, piece_recv,
):
    li = lax.axis_index("light")
    vi = lax.axis_index("view")
    chip, core = li // 2, li % 2
    chips = light_count // 2
    cells, planes, lanes = x_hbm.shape
    chunks = planes // ROWS
    rows = planes // view_count
    per_chunk = ROWS // rows
    steps = cells // BLOCK
    vx = vi // per_chunk

    def load(k):
        z0 = pl.multiple_of(((vx + TURN[k]) % chunks) * ROWS, ROWS)
        return pltpu.make_async_copy(x_hbm.at[:, pl.ds(z0, ROWS), :], xv.at[k], x_sem.at[k])

    def sib_copy(k):
        return pltpu.make_async_remote_copy(
            src_ref=own_sum.at[k], dst_ref=sib_sum.at[k], send_sem=sib_send.at[k], recv_sem=sib_recv.at[k],
            device_id=(chip * 2 + 1, vi), device_id_type=MESH)

    def low_copy(k, to_chip, to_core):
        return pltpu.make_async_remote_copy(
            src_ref=chip_sum.at[k], dst_ref=low_sum.at[chip, k],
            send_sem=low_send.at[to_chip - 1, to_core, k], recv_sem=low_recv.at[chip, k],
            device_id=(to_chip * 2 + to_core, vi), device_id_type=MESH)

    def low_arrival(k, from_chip):
        return pltpu.make_async_remote_copy(
            src_ref=chip_sum.at[k], dst_ref=low_sum.at[from_chip, k],
            send_sem=low_send.at[0, 0, k], recv_sem=low_recv.at[from_chip, k],
            device_id=(from_chip * 2 + 1, vi), device_id_type=MESH)

    def piece_copy(k, d, j):
        return pltpu.make_async_remote_copy(
            src_ref=piece.at[k, d], dst_ref=got.at[vi], send_sem=piece_send, recv_sem=piece_recv,
            device_id=(li, j), device_id_type=MESH)

    def all_pieces():
        others = pl.ds(0, view_count - 1)
        return pltpu.make_async_remote_copy(
            src_ref=got.at[others], dst_ref=got.at[others], send_sem=piece_send, recv_sem=piece_recv,
            device_id=(li, (vi + 1) % view_count), device_id_type=MESH)

    for k in range(chunks):
        load(k).start()
    coef_copy = pltpu.make_async_copy(coef_hbm, coef_s, coef_sem)
    coef_copy.start()

    barrier = pltpu.get_barrier_semaphore()

    @pl.when(core == 1)
    def _():
        pl.semaphore_signal(barrier, inc=1, device_id=(li - 1, vi), device_id_type=MESH)

    for c in range(chips - 1):
        @pl.when(c < chip)
        def _():
            pl.semaphore_signal(barrier, inc=1, device_id=(2 * c + 1, vi), device_id_type=MESH)

    for other in range(1, view_count):
        pl.semaphore_signal(barrier, inc=1, device_id=(li, (vi + other) % view_count), device_id_type=MESH)

    row = lax.broadcasted_iota(jnp.int32, (ROWS, lanes), 0)
    def sum_up(k):
        load(k).wait()
        acc = jnp.zeros((steps, BLOCK * ROWS), F32)
        for p in range(steps):
            xb = xv[k, p * BLOCK : (p + 1) * BLOCK].reshape(BLOCK * ROWS, lanes)
            pick = jnp.where(row == p, 1.0, 0.0).astype(BF16)[:steps]
            acc = acc + lax.dot_general(pick, xb, (((1,), (1,)), ((), ())), preferred_element_type=F32)
        own_sum[k, 0:steps] = acc[:, : HALF * ROWS]
        own_sum[k, steps:] = acc[:, HALF * ROWS :]

    def meet():
        pl.semaphore_wait(barrier, (view_count - 1) + jnp.where(core == 0, 1, 2 * (chips - 1 - chip)))

    def share(ks):
        @pl.when(core == 0)
        def _():
            for k in ks:
                sib_copy(k).start()

    def lower(ks):
        @pl.when(core == 1)
        def _():
            for k in ks:
                sib_copy(k).wait_recv()
                chip_sum[k] = own_sum[k] + sib_sum[k]
                for to_chip in range(1, chips):
                    @pl.when(to_chip > chip)
                    def _():
                        for to_core in range(2):
                            low_copy(k, to_chip, to_core).start()

    view_scale = -LOG2E * 2.0 / view_total
    light_scale = -LOG2E * 2.0 / light_total
    r = lax.broadcasted_iota(jnp.int32, (lanes, lanes), 0)
    c = lax.broadcasted_iota(jnp.int32, (lanes, lanes), 1)
    before = jnp.where(r < c, 1.0, 0.0).astype(BF16)
    def near_side(k):
        def local(b, clear):
            xb = xv[k, pl.ds(b * BLOCK, BLOCK)].reshape(BLOCK * ROWS, lanes)
            depth = jnp.dot(xb, before, preferred_element_type=F32).reshape(BLOCK, ROWS, lanes)
            xb = xb.reshape(BLOCK, ROWS, lanes)
            for v in range(BLOCK):
                x = xb[v].astype(F32)
                beyond = clear * jnp.exp2(view_scale * x)
                a = clear - beyond
                clear = beyond
                xf[k, b * BLOCK + v] = x
                alpha[k, b * BLOCK + v] = a
                lit_alpha[k, b * BLOCK + v] = a * jnp.exp2(light_scale * depth[v])
            return clear

        clears[k] = lax.fori_loop(0, steps, local, jnp.ones((ROWS, lanes), F32), unroll=8)

    def light_up(k):
        upper[...] = jnp.zeros_like(upper)

        @pl.when(core == 1)
        def _():
            upper[...] += sib_sum[k]

        for c in range(chips - 1):
            @pl.when(c < chip)
            def _():
                low_arrival(k, c).wait_recv()
                upper[...] += low_sum[c, k]

        dim_t[...] = jnp.transpose(jnp.exp2(light_scale * upper[...]) * (1.0 / AMBIENT))

        def spread(p):
            for h in range(2):
                at = jnp.full((HALF * ROWS, 2 * steps), h * steps, jnp.int32) + p
                near = jnp.take_along_axis(dim_t[...], jnp.broadcast_to(at[:, :1], (HALF * ROWS, lanes)), axis=1)
                dims[p % 2, h * HALF : (h + 1) * HALF] = near.reshape(HALF, ROWS, lanes)

        def lighted(p, carry):
            m0, m1, m2, m3 = carry
            spread(p)
            for v in range(BLOCK):
                x = xf[k, p * BLOCK + v]
                a = alpha[k, p * BLOCK + v] + lit_alpha[k, p * BLOCK + v] * dims[p % 2, v]
                m0 = m0 + a
                a = a * x
                m1 = m1 + a
                a = a * x
                m2 = m2 + a
                a = a * x
                m3 = m3 + a
            return m0, m1, m2, m3

        zero = jnp.zeros((ROWS, lanes), F32)
        sums = lax.fori_loop(0, steps, lighted, (zero, zero, zero, zero), unroll=8)
        parts = []
        for ch in range(3):
            t = coef_s[ch, 0] * sums[0] + coef_s[ch, 1] * sums[1] + coef_s[ch, 2] * sums[2] + coef_s[ch, 3] * sums[3]
            parts.append(AMBIENT * t)
        parts.append(clears[k])
        to = ((vx + TURN[k]) % chunks) * per_chunk
        for d in range(per_chunk):
            mine = jnp.concatenate([p[d * rows : (d + 1) * rows] for p in parts], axis=0)
            piece[k, d] = mine
            j = to + d

            @pl.when(j == vi)
            def _():
                got[vi] = mine

            @pl.when(j != vi)
            def _():
                piece_copy(k, d, j).start()

    for step in ORDER:
        name, ks = step[0], [int(q) for q in step[1:]]
        if name == "M":
            meet()
        elif name == "W":
            coef_copy.wait()
        elif name in "SC":
            (share if name == "S" else lower)(ks)
        else:
            for k in ks:
                {"A": sum_up, "L": near_side, "B": light_up}[name](k)

    all_pieces().wait_recv()
    half = lax.broadcasted_iota(jnp.int32, (2 * rows, lanes), 0)
    clear = jnp.ones((2 * rows, lanes), F32)
    total = [jnp.zeros((2 * rows, lanes), F32) for _ in range(2)]
    for i in range(view_count):
        first, second = got[i, : 2 * rows], got[i, 2 * rows :]
        total[0] = total[0] + clear * first
        total[1] = total[1] + clear * second
        clear = clear * jnp.where(half < rows, pltpu.roll(second, rows, 0), second)
    out_ref[0] = total[0][:rows]
    out_ref[1] = total[0][rows:]
    out_ref[2] = total[1][:rows]

    all_pieces().wait_send()

    @pl.when(core == 0)
    def _():
        for k in range(chunks):
            sib_copy(k).wait_send()

    @pl.when(core == 1)
    def _():
        for k in range(chunks):
            for to_chip in range(1, chips):
                @pl.when(to_chip > chip)
                def _():
                    for to_core in range(2):
                        low_copy(k, to_chip, to_core).wait_send()


def body(density, color_coef):
    cells, planes, lanes = density.shape
    light_count = lax.axis_size("light")
    view_count = lax.axis_size("view")
    chips = light_count // 2
    chunks = planes // ROWS
    rows = planes // view_count
    per_chunk = ROWS // rows
    dma = pltpu.SemaphoreType.DMA
    return pl.pallas_call(
        functools.partial(kernel, lanes * light_count, cells * view_count, light_count, view_count),
        out_shape=pltpu.VMEM((3, rows, lanes), F32),
        in_specs=[pl.BlockSpec(memory_space=pl.ANY), pl.BlockSpec(memory_space=pl.ANY)],
        out_specs=pl.BlockSpec(memory_space=pltpu.VMEM),
        scratch_shapes=[
            pltpu.VMEM((chunks, cells, ROWS, lanes), BF16),
            pltpu.SMEM((3, 4), F32),
            pltpu.VMEM((chunks, ROWS, lanes), F32),
            pltpu.VMEM((chunks, ROWS, lanes), F32),
            pltpu.VMEM((chunks, ROWS, lanes), F32),
            pltpu.VMEM((chips - 1, chunks, ROWS, lanes), F32),
            pltpu.VMEM((ROWS, lanes), F32),
            pltpu.VMEM((HALF * ROWS, ROWS), F32),
            pltpu.VMEM((2, BLOCK, ROWS, lanes), F32),
            pltpu.VMEM((chunks, cells, ROWS, lanes), F32),
            pltpu.VMEM((chunks, cells, ROWS, lanes), F32),
            pltpu.VMEM((chunks, cells, ROWS, lanes), F32),
            pltpu.VMEM((chunks, ROWS, lanes), F32),
            pltpu.VMEM((chunks, per_chunk, 4 * rows, lanes), F32),
            pltpu.VMEM((view_count, 4 * rows, lanes), F32),
            dma((chunks,)),
            dma,
            dma((chunks,)),
            dma((chunks,)),
            dma((chips - 1, 2, chunks)),
            dma((chips - 1, chunks)),
            dma,
            dma,
        ],
        compiler_params=pltpu.CompilerParams(collective_id=0, has_side_effects=True),
    )(density, color_coef)


def solution(mesh):
    placed = (P("view", None, "light"), P())
    return jax.shard_map(
        body, mesh=mesh, in_specs=placed, out_specs=P(None, "view", "light"), check_vma=False
    )
```

```python
import functools
import math

import jax
import jax.numpy as jnp
from jax import lax
from jax.experimental import pallas as pl
from jax.experimental.pallas import tpu as pltpu
from jax.sharding import PartitionSpec as P

F32 = jnp.float32
BF16 = jnp.bfloat16
LOG2E = math.log2(math.e)
ROWS = 16
BLOCK = 16
HALF = BLOCK // 2
TURN = (2, 1, 3, 0)
AMBIENT = 0.3
ORDER = ("A0123", "L0", "M", "S0123", "L1", "C0123", "L23", "W", "B0123")
MESH = pl.DeviceIdType.MESH


def kernel(
    light_total, view_total, light_count, view_count,
    x_hbm, coef_hbm, out_ref,
    xv, coef_s, own_sum, sib_sum, chip_sum, low_sum, upper, picks, alpha, lit_alpha, clears, piece, got,
    x_sem, coef_sem, sib_send, sib_recv, low_send, low_recv, piece_send, piece_recv, lines,
):
    li = lax.axis_index("light")
    vi = lax.axis_index("view")
    chip, core = li // 2, li % 2
    chips = light_count // 2
    cells, planes, lanes = x_hbm.shape
    chunks = planes // ROWS
    rows = planes // view_count
    per_chunk = ROWS // rows
    steps = cells // BLOCK
    vx, vy = vi // per_chunk, vi % per_chunk

    def load(k):
        z0 = pl.multiple_of(((vx + TURN[k]) % chunks) * ROWS, ROWS)
        return pltpu.make_async_copy(x_hbm.at[:, pl.ds(z0, ROWS), :], xv.at[k], x_sem.at[k])

    def sib_copy(k):
        return pltpu.make_async_remote_copy(
            src_ref=own_sum.at[k], dst_ref=sib_sum.at[k], send_sem=sib_send.at[k], recv_sem=sib_recv.at[k],
            device_id=(chip * 2 + 1, vi), device_id_type=MESH)

    def low_copy(k, to_chip, to_core):
        return pltpu.make_async_remote_copy(
            src_ref=chip_sum.at[k], dst_ref=low_sum.at[chip, k],
            send_sem=low_send.at[to_chip - 1, to_core, k], recv_sem=low_recv.at[chip, k],
            device_id=(to_chip * 2 + to_core, vi), device_id_type=MESH)

    def low_arrival(k, from_chip):
        return pltpu.make_async_remote_copy(
            src_ref=chip_sum.at[k], dst_ref=low_sum.at[from_chip, k],
            send_sem=low_send.at[0, 0, k], recv_sem=low_recv.at[from_chip, k],
            device_id=(from_chip * 2 + 1, vi), device_id_type=MESH)

    def piece_copy(k, d, j):
        return pltpu.make_async_remote_copy(
            src_ref=piece.at[k, d], dst_ref=got.at[vi], send_sem=piece_send, recv_sem=piece_recv,
            device_id=(li, j), device_id_type=MESH)

    def all_pieces():
        others = pl.ds(0, view_count - 1)
        return pltpu.make_async_remote_copy(
            src_ref=got.at[others], dst_ref=got.at[others], send_sem=piece_send, recv_sem=piece_recv,
            device_id=(li, (vi + 1) % view_count), device_id_type=MESH)

    for k in range(chunks):
        load(k).start()
    coef_copy = pltpu.make_async_copy(coef_hbm, coef_s, coef_sem)
    coef_copy.start()

    barrier = pltpu.get_barrier_semaphore()

    @pl.when(core == 1)
    def _():
        pl.semaphore_signal(barrier, inc=1, device_id=(li - 1, vi), device_id_type=MESH)

    for c in range(chips - 1):
        @pl.when(c < chip)
        def _():
            pl.semaphore_signal(barrier, inc=1, device_id=(2 * c + 1, vi), device_id_type=MESH)

    for turn in range(1, chunks):
        for j in (((vx + turn) % chunks) * per_chunk + vy, vx * per_chunk + (vy + turn) % per_chunk):
            pl.semaphore_signal(barrier, inc=1, device_id=(li, j), device_id_type=MESH)

    term_row = lax.broadcasted_iota(jnp.int32, (3 * ROWS, lanes), 0) % ROWS
    for q in range(ROWS):
        picks[q] = jnp.where(term_row == q, 1.0, 0.0).astype(BF16)

    row = lax.broadcasted_iota(jnp.int32, (ROWS, lanes), 0)
    def sum_up(k):
        load(k).wait()
        acc = jnp.zeros((steps, BLOCK * ROWS), F32)
        for p in range(steps):
            xb = xv[k, p * BLOCK : (p + 1) * BLOCK].reshape(BLOCK * ROWS, lanes)
            pick = jnp.where(row == p, 1.0, 0.0).astype(BF16)[:steps]
            acc = acc + lax.dot_general(pick, xb, (((1,), (1,)), ((), ())), preferred_element_type=F32)
        own_sum[k, 0:steps] = acc[:, : HALF * ROWS]
        own_sum[k, steps:] = acc[:, HALF * ROWS :]

    def meet():
        pl.semaphore_wait(barrier, chunks + per_chunk - 2 + jnp.where(core == 0, 1, 2 * (chips - 1 - chip)))
        for turn in range(1, per_chunk):
            j = vx * per_chunk + (vy + turn) % per_chunk
            pl.semaphore_signal(lines, inc=1, device_id=(li, j), device_id_type=MESH)

    def share(ks):
        @pl.when(core == 0)
        def _():
            for k in ks:
                sib_copy(k).start()

    def lower(ks):
        @pl.when(core == 1)
        def _():
            for k in ks:
                sib_copy(k).wait_recv()
                chip_sum[k] = own_sum[k] + sib_sum[k]
                for to_chip in range(1, chips):
                    @pl.when(to_chip > chip)
                    def _():
                        for to_core in range(2):
                            low_copy(k, to_chip, to_core).start()

    view_scale = -LOG2E * 2.0 / view_total
    light_scale = -LOG2E * 2.0 / light_total
    r = lax.broadcasted_iota(jnp.int32, (lanes, lanes), 0)
    c = lax.broadcasted_iota(jnp.int32, (lanes, lanes), 1)
    before = jnp.where(r < c, 1.0, 0.0).astype(BF16)
    def near_side(k):
        def local(b, clear):
            xb = xv[k, pl.ds(b * BLOCK, BLOCK)].reshape(BLOCK * ROWS, lanes)
            depth = jnp.dot(xb, before, preferred_element_type=F32).reshape(BLOCK, ROWS, lanes)
            xb = xb.reshape(BLOCK, ROWS, lanes)
            for v in range(BLOCK):
                x = xb[v].astype(F32)
                beyond = clear * jnp.exp2(view_scale * x)
                a = clear - beyond
                clear = beyond
                alpha[k, b * BLOCK + v] = a
                lit_alpha[k, b * BLOCK + v] = a * jnp.exp2(light_scale * depth[v])
            return clear

        clears[k] = lax.fori_loop(0, steps, local, jnp.ones((ROWS, lanes), F32), unroll=8)

    def light_up(k):
        upper[...] = jnp.zeros_like(upper)

        @pl.when(core == 1)
        def _():
            upper[...] += sib_sum[k]

        for c in range(chips - 1):
            @pl.when(c < chip)
            def _():
                low_arrival(k, c).wait_recv()
                upper[...] += low_sum[c, k]

        rest = jnp.exp2(light_scale * upper[...]) * (1.0 / AMBIENT)
        terms = []
        for _ in range(3):
            term = rest.astype(BF16).astype(F32)
            rest = rest - term
            terms.append(term)
        dim_t = jnp.transpose(jnp.concatenate(terms, axis=0)).astype(BF16)
        m0, m1, m2, m3 = (jnp.zeros((ROWS, lanes), F32) for _ in range(4))
        for p in range(steps):
            for h in range(2):
                near = jnp.dot(dim_t, picks[p + h * steps], preferred_element_type=F32).reshape(HALF, ROWS, lanes)
                for i in range(HALF):
                    v = p * BLOCK + h * HALF + i
                    x = xv[k, v].astype(F32)
                    a = alpha[k, v] + lit_alpha[k, v] * near[i]
                    m0 = m0 + a
                    a = a * x
                    m1 = m1 + a
                    a = a * x
                    m2 = m2 + a
                    a = a * x
                    m3 = m3 + a
        sums = (m0, m1, m2, m3)
        parts = []
        for ch in range(3):
            t = coef_s[ch, 0] * sums[0] + coef_s[ch, 1] * sums[1] + coef_s[ch, 2] * sums[2] + coef_s[ch, 3] * sums[3]
            parts.append(AMBIENT * t)
        parts.append(clears[k])
        if k == 0:
            pl.semaphore_wait(lines, per_chunk - 1)
        to = ((vx + TURN[k]) % chunks) * per_chunk
        for d in range(per_chunk):
            mine = jnp.concatenate([p[d * rows : (d + 1) * rows] for p in parts], axis=0)
            piece[k, d] = mine
            j = to + d

            @pl.when(j == vi)
            def _():
                got[vi] = mine

            @pl.when(j != vi)
            def _():
                piece_copy(k, d, j).start()

    for step in ORDER:
        name, ks = step[0], [int(q) for q in step[1:]]
        if name == "M":
            meet()
        elif name == "W":
            coef_copy.wait()
        elif name in "SC":
            (share if name == "S" else lower)(ks)
        else:
            for k in ks:
                {"A": sum_up, "L": near_side, "B": light_up}[name](k)

    all_pieces().wait_recv()
    half = lax.broadcasted_iota(jnp.int32, (2 * rows, lanes), 0)
    clear = jnp.ones((2 * rows, lanes), F32)
    total = [jnp.zeros((2 * rows, lanes), F32) for _ in range(2)]
    for i in range(view_count):
        first, second = got[i, : 2 * rows], got[i, 2 * rows :]
        total[0] = total[0] + clear * first
        total[1] = total[1] + clear * second
        clear = clear * jnp.where(half < rows, pltpu.roll(second, rows, 0), second)
    out_ref[0] = total[0][:rows]
    out_ref[1] = total[0][rows:]
    out_ref[2] = total[1][:rows]

    all_pieces().wait_send()

    @pl.when(core == 0)
    def _():
        for k in range(chunks):
            sib_copy(k).wait_send()

    @pl.when(core == 1)
    def _():
        for k in range(chunks):
            for to_chip in range(1, chips):
                @pl.when(to_chip > chip)
                def _():
                    for to_core in range(2):
                        low_copy(k, to_chip, to_core).wait_send()


def body(density, color_coef):
    cells, planes, lanes = density.shape
    light_count = lax.axis_size("light")
    view_count = lax.axis_size("view")
    chips = light_count // 2
    chunks = planes // ROWS
    rows = planes // view_count
    per_chunk = ROWS // rows
    dma = pltpu.SemaphoreType.DMA
    return pl.pallas_call(
        functools.partial(kernel, lanes * light_count, cells * view_count, light_count, view_count),
        out_shape=pltpu.VMEM((3, rows, lanes), F32),
        in_specs=[pl.BlockSpec(memory_space=pl.ANY), pl.BlockSpec(memory_space=pl.ANY)],
        out_specs=pl.BlockSpec(memory_space=pltpu.VMEM),
        scratch_shapes=[
            pltpu.VMEM((chunks, cells, ROWS, lanes), BF16),
            pltpu.SMEM((3, 4), F32),
            pltpu.VMEM((chunks, ROWS, lanes), F32),
            pltpu.VMEM((chunks, ROWS, lanes), F32),
            pltpu.VMEM((chunks, ROWS, lanes), F32),
            pltpu.VMEM((chips - 1, chunks, ROWS, lanes), F32),
            pltpu.VMEM((ROWS, lanes), F32),
            pltpu.VMEM((ROWS, 3 * ROWS, lanes), BF16),
            pltpu.VMEM((chunks, cells, ROWS, lanes), F32),
            pltpu.VMEM((chunks, cells, ROWS, lanes), F32),
            pltpu.VMEM((chunks, ROWS, lanes), F32),
            pltpu.VMEM((chunks, per_chunk, 4 * rows, lanes), F32),
            pltpu.VMEM((view_count, 4 * rows, lanes), F32),
            dma((chunks,)),
            dma,
            dma((chunks,)),
            dma((chunks,)),
            dma((chips - 1, 2, chunks)),
            dma((chips - 1, chunks)),
            dma,
            dma,
            pltpu.SemaphoreType.REGULAR,
        ],
        compiler_params=pltpu.CompilerParams(collective_id=0, has_side_effects=True),
    )(density, color_coef)


def solution(mesh):
    placed = (P("view", None, "light"), P())
    return jax.shard_map(
        body, mesh=mesh, in_specs=placed, out_specs=P(None, "view", "light"), check_vma=False
    )
```

```python
import functools
import math

import jax
import jax.numpy as jnp
from jax import lax
from jax.experimental import pallas as pl
from jax.experimental.pallas import tpu as pltpu
from jax.sharding import PartitionSpec as P

F32 = jnp.float32
BF16 = jnp.bfloat16
LOG2E = math.log2(math.e)
ROWS = 16
BLOCK = 16
HALF = BLOCK // 2
TURN = (0, 1, 3, 2)
GROUPS = ((0, 1), (1, 3))
AMBIENT = 0.3
ORDER = ("A0123", "L0", "M", "S", "L1", "D1", "D2", "D3", "L23", "W", "B0123")
MESH = pl.DeviceIdType.MESH


def kernel(
    light_total, view_total, light_count, view_count,
    x_hbm, coef_hbm, out_ref,
    xv, coef_s, own_sum, sib_sum, chip_sum, low_sum, upper, picks, alpha, lit_alpha, clears, piece, got,
    x_sem, coef_sem, sib_send, sib_recv, low_send, low_recv, piece_send, piece_recv, lines,
):
    li = lax.axis_index("light")
    vi = lax.axis_index("view")
    chip, core = li // 2, li % 2
    chips = light_count // 2
    cells, planes, lanes = x_hbm.shape
    chunks = planes // ROWS
    rows = planes // view_count
    per_chunk = ROWS // rows
    steps = cells // BLOCK
    vx, vy = vi // per_chunk, vi % per_chunk

    def load(k):
        z0 = TURN[k] * ROWS
        return pltpu.make_async_copy(x_hbm.at[:, pl.ds(z0, ROWS), :], xv.at[k], x_sem.at[k])

    def sib_copy(g):
        ks = pl.ds(*GROUPS[g])
        return pltpu.make_async_remote_copy(
            src_ref=own_sum.at[ks], dst_ref=sib_sum.at[ks], send_sem=sib_send.at[g], recv_sem=sib_recv.at[g],
            device_id=(chip * 2 + 1, vi), device_id_type=MESH)

    def low_copy(g, by, to_core):
        ks = pl.ds(*GROUPS[g])
        return pltpu.make_async_remote_copy(
            src_ref=chip_sum.at[ks], dst_ref=low_sum.at[chip, ks],
            send_sem=low_send.at[by - 1, to_core, g], recv_sem=low_recv.at[chip, g],
            device_id=((chip + by) * 2 + to_core, vi), device_id_type=MESH)

    def low_arrival(g, c):
        ks = pl.ds(*GROUPS[g])
        return pltpu.make_async_remote_copy(
            src_ref=chip_sum.at[ks], dst_ref=low_sum.at[c, ks],
            send_sem=low_send.at[0, 0, g], recv_sem=low_recv.at[c, g],
            device_id=(c * 2 + 1, vi), device_id_type=MESH)

    def piece_copy(k, d, j):
        return pltpu.make_async_remote_copy(
            src_ref=piece.at[k, d], dst_ref=got.at[vi], send_sem=piece_send, recv_sem=piece_recv,
            device_id=(li, j), device_id_type=MESH)

    def all_pieces():
        others = pl.ds(0, view_count - 1)
        return pltpu.make_async_remote_copy(
            src_ref=got.at[others], dst_ref=got.at[others], send_sem=piece_send, recv_sem=piece_recv,
            device_id=(li, (vi + 1) % view_count), device_id_type=MESH)

    for k in range(chunks):
        load(k).start()
    coef_copy = pltpu.make_async_copy(coef_hbm, coef_s, coef_sem)
    coef_copy.start()

    barrier = pltpu.get_barrier_semaphore()

    @pl.when(core == 1)
    def _():
        pl.semaphore_signal(barrier, inc=1, device_id=(li - 1, vi), device_id_type=MESH)

    for c in range(chips - 1):
        @pl.when(c < chip)
        def _():
            pl.semaphore_signal(barrier, inc=1, device_id=(2 * c + 1, vi), device_id_type=MESH)

    for turn in range(1, chunks):
        for j in (((vx + turn) % chunks) * per_chunk + vy, vx * per_chunk + (vy + turn) % per_chunk):
            pl.semaphore_signal(barrier, inc=1, device_id=(li, j), device_id_type=MESH)

    term_row = lax.broadcasted_iota(jnp.int32, (3 * ROWS, lanes), 0) % ROWS
    for q in range(ROWS):
        picks[q] = jnp.where(term_row == q, 1.0, 0.0).astype(BF16)

    row = lax.broadcasted_iota(jnp.int32, (ROWS, lanes), 0)
    def sum_up(k):
        load(k).wait()
        acc = jnp.zeros((steps, BLOCK * ROWS), F32)
        for p in range(steps):
            xb = xv[k, p * BLOCK : (p + 1) * BLOCK].reshape(BLOCK * ROWS, lanes)
            pick = jnp.where(row == p, 1.0, 0.0).astype(BF16)[:steps]
            acc = acc + lax.dot_general(pick, xb, (((1,), (1,)), ((), ())), preferred_element_type=F32)
        own_sum[k, 0:steps] = acc[:, : HALF * ROWS]
        own_sum[k, steps:] = acc[:, HALF * ROWS :]

    def meet():
        pl.semaphore_wait(barrier, chunks + per_chunk - 2 + jnp.where(core == 0, 1, 2 * (chips - 1 - chip)))

        for turn in range(1, per_chunk):
            j = vx * per_chunk + (vy + turn) % per_chunk
            pl.semaphore_signal(lines, inc=1, device_id=(li, j), device_id_type=MESH)

    def share():
        @pl.when(core == 0)
        def _():
            for g in range(len(GROUPS)):
                sib_copy(g).start()

    def lower(by):
        if by == 1:
            @pl.when(core == 1)
            def _():
                for g in range(len(GROUPS)):
                    sib_copy(g).wait_recv()
                chip_sum[...] = own_sum[...] + sib_sum[...]

        @pl.when((core == 1) & (chip + by < chips))
        def _():
            for g in range(len(GROUPS)):
                for to_core in range(2):
                    low_copy(g, by, to_core).start()

    view_scale = -LOG2E * 2.0 / view_total
    light_scale = -LOG2E * 2.0 / light_total
    r = lax.broadcasted_iota(jnp.int32, (lanes, lanes), 0)
    c = lax.broadcasted_iota(jnp.int32, (lanes, lanes), 1)
    before = jnp.where(r < c, 1.0, 0.0).astype(BF16)
    def near_side(k):
        def local(b, clear):
            xb = xv[k, pl.ds(b * BLOCK, BLOCK)].reshape(BLOCK * ROWS, lanes)
            depth = jnp.dot(xb, before, preferred_element_type=F32).reshape(BLOCK, ROWS, lanes)
            xb = xb.reshape(BLOCK, ROWS, lanes)
            for v in range(BLOCK):
                x = xb[v].astype(F32)
                beyond = clear * jnp.exp2(view_scale * x)
                a = clear - beyond
                clear = beyond
                alpha[k, b * BLOCK + v] = a
                lit_alpha[k, b * BLOCK + v] = a * jnp.exp2(light_scale * depth[v])
            return clear

        clears[k] = lax.fori_loop(0, steps, local, jnp.ones((ROWS, lanes), F32), unroll=8)

    def light_up(k):
        @pl.when(core == 0)
        def _():
            upper[...] = jnp.zeros_like(upper)

        @pl.when(core == 1)
        def _():
            upper[...] = sib_sum[k]

        for c in range(chips - 1):
            @pl.when(c < chip)
            def _():
                if k < len(GROUPS):
                    low_arrival(k, c).wait_recv()
                upper[...] += low_sum[c, k]

        rest = jnp.exp2(light_scale * upper[...]) * (1.0 / AMBIENT)
        terms = []
        for _ in range(3):
            term = rest.astype(BF16).astype(F32)
            rest = rest - term
            terms.append(term)
        dim_t = jnp.transpose(jnp.concatenate(terms, axis=0)).astype(BF16)
        m0, m1, m2, m3 = (jnp.zeros((ROWS, lanes), F32) for _ in range(4))
        for p in range(steps):
            for h in range(2):
                near = jnp.dot(dim_t, picks[p + h * steps], preferred_element_type=F32).reshape(HALF, ROWS, lanes)
                for i in range(HALF):
                    v = p * BLOCK + h * HALF + i
                    x = xv[k, v].astype(F32)
                    a = alpha[k, v] + lit_alpha[k, v] * near[i]
                    m0 = m0 + a
                    a = a * x
                    m1 = m1 + a
                    a = a * x
                    m2 = m2 + a
                    a = a * x
                    m3 = m3 + a
        sums = (m0, m1, m2, m3)
        parts = []
        for ch in range(3):
            t = coef_s[ch, 0] * sums[0] + coef_s[ch, 1] * sums[1] + coef_s[ch, 2] * sums[2] + coef_s[ch, 3] * sums[3]
            parts.append(AMBIENT * t)
        parts.append(clears[k])
        if k == 0:
            pl.semaphore_wait(lines, per_chunk - 1)
        to = TURN[k] * per_chunk
        for d in range(per_chunk):
            mine = jnp.concatenate([p[d * rows : (d + 1) * rows] for p in parts], axis=0)
            piece[k, d] = mine
            j = to + d

            @pl.when(j == vi)
            def _():
                got[vi] = mine

            @pl.when(j != vi)
            def _():
                piece_copy(k, d, j).start()

    one = {"M": meet, "S": share, "W": coef_copy.wait}
    each = {"A": sum_up, "D": lower, "L": near_side, "B": light_up}
    for step in ORDER:
        if step in one:
            one[step]()
        else:
            for q in step[1:]:
                each[step[0]](int(q))

    all_pieces().wait_recv()
    half = lax.broadcasted_iota(jnp.int32, (2 * rows, lanes), 0)
    clear = jnp.ones((2 * rows, lanes), F32)
    total = [jnp.zeros((2 * rows, lanes), F32) for _ in range(2)]
    for i in range(view_count):
        first, second = got[i, : 2 * rows], got[i, 2 * rows :]
        total[0] = total[0] + clear * first
        total[1] = total[1] + clear * second
        clear = clear * jnp.where(half < rows, pltpu.roll(second, rows, 0), second)
    out_ref[0] = total[0][:rows]
    out_ref[1] = total[0][rows:]
    out_ref[2] = total[1][:rows]

    all_pieces().wait_send()

    @pl.when(core == 0)
    def _():
        for g in range(len(GROUPS)):
            sib_copy(g).wait_send()

    for by in range(1, chips):
        @pl.when((core == 1) & (chip + by < chips))
        def _():
            for g in range(len(GROUPS)):
                for to_core in range(2):
                    low_copy(g, by, to_core).wait_send()


def body(density, color_coef):
    cells, planes, lanes = density.shape
    light_count = lax.axis_size("light")
    view_count = lax.axis_size("view")
    chips = light_count // 2
    chunks = planes // ROWS
    rows = planes // view_count
    per_chunk = ROWS // rows
    dma = pltpu.SemaphoreType.DMA
    return pl.pallas_call(
        functools.partial(kernel, lanes * light_count, cells * view_count, light_count, view_count),
        out_shape=pltpu.VMEM((3, rows, lanes), F32),
        in_specs=[pl.BlockSpec(memory_space=pl.ANY), pl.BlockSpec(memory_space=pl.ANY)],
        out_specs=pl.BlockSpec(memory_space=pltpu.VMEM),
        scratch_shapes=[
            pltpu.VMEM((chunks, cells, ROWS, lanes), BF16),
            pltpu.SMEM((3, 4), F32),
            pltpu.VMEM((chunks, ROWS, lanes), F32),
            pltpu.VMEM((chunks, ROWS, lanes), F32),
            pltpu.VMEM((chunks, ROWS, lanes), F32),
            pltpu.VMEM((chips - 1, chunks, ROWS, lanes), F32),
            pltpu.VMEM((ROWS, lanes), F32),
            pltpu.VMEM((ROWS, 3 * ROWS, lanes), BF16),
            pltpu.VMEM((chunks, cells, ROWS, lanes), F32),
            pltpu.VMEM((chunks, cells, ROWS, lanes), F32),
            pltpu.VMEM((chunks, ROWS, lanes), F32),
            pltpu.VMEM((chunks, per_chunk, 4 * rows, lanes), F32),
            pltpu.VMEM((view_count, 4 * rows, lanes), F32),
            dma((chunks,)),
            dma,
            dma((len(GROUPS),)),
            dma((len(GROUPS),)),
            dma((chips - 1, 2, len(GROUPS))),
            dma((chips - 1, len(GROUPS))),
            dma,
            dma,
            pltpu.SemaphoreType.REGULAR,
        ],
        compiler_params=pltpu.CompilerParams(collective_id=0, has_side_effects=True),
    )(density, color_coef)


def solution(mesh):
    placed = (P("view", None, "light"), P())
    return jax.shard_map(
        body, mesh=mesh, in_specs=placed, out_specs=P(None, "view", "light"), check_vma=False
    )
```

```python
import functools
import math

import jax
import jax.numpy as jnp
from jax import lax
from jax.experimental import pallas as pl
from jax.experimental.pallas import tpu as pltpu
from jax.sharding import PartitionSpec as P

F32 = jnp.float32
BF16 = jnp.bfloat16
LOG2E = math.log2(math.e)
ROWS = 16
BLOCK = 16
HALF = BLOCK // 2
HROWS = ROWS // 2
TURN = (0, 1, 3, 2)
GROUPS = ((0, 1), (1, 3))
AMBIENT = 0.3
MESH = pl.DeviceIdType.MESH


def kernel(
    light_total, view_total, light_count, view_count,
    x_hbm, coef_hbm, out_ref,
    xv, coef_s, own_sum, sib_sum, chip_sum, low_sum, upper, picks, dims, alpha, lit_alpha, clears, piece, got,
    x_sem, coef_sem, sib_send, sib_recv, low_send, low_recv, piece_send, piece_recv, lines,
):
    li = lax.axis_index("light")
    vi = lax.axis_index("view")
    chip, core = li // 2, li % 2
    chips = light_count // 2
    cells, planes, lanes = x_hbm.shape
    chunks = planes // ROWS
    rows = planes // view_count
    per_chunk = ROWS // rows
    steps = cells // BLOCK
    vx, vy = vi // per_chunk, vi % per_chunk

    def load(k):
        z0 = TURN[k] * ROWS
        return pltpu.make_async_copy(x_hbm.at[:, pl.ds(z0, ROWS), :], xv.at[k], x_sem.at[k])

    def sib_copy(g):
        ks = pl.ds(*GROUPS[g])
        return pltpu.make_async_remote_copy(
            src_ref=own_sum.at[ks], dst_ref=sib_sum.at[ks], send_sem=sib_send.at[g], recv_sem=sib_recv.at[g],
            device_id=(chip * 2 + 1, vi), device_id_type=MESH)

    def low_copy(g, by, to_core):
        ks = pl.ds(*GROUPS[g])
        return pltpu.make_async_remote_copy(
            src_ref=chip_sum.at[ks], dst_ref=low_sum.at[chip, ks],
            send_sem=low_send.at[by - 1, to_core, g], recv_sem=low_recv.at[chip, g],
            device_id=((chip + by) * 2 + to_core, vi), device_id_type=MESH)

    def low_arrival(g, c):
        ks = pl.ds(*GROUPS[g])
        return pltpu.make_async_remote_copy(
            src_ref=chip_sum.at[ks], dst_ref=low_sum.at[c, ks],
            send_sem=low_send.at[0, 0, g], recv_sem=low_recv.at[c, g],
            device_id=(c * 2 + 1, vi), device_id_type=MESH)

    def piece_copy(k, d, j):
        return pltpu.make_async_remote_copy(
            src_ref=piece.at[k, d], dst_ref=got.at[vi], send_sem=piece_send, recv_sem=piece_recv,
            device_id=(li, j), device_id_type=MESH)

    def all_pieces():
        others = pl.ds(0, view_count - 1)
        return pltpu.make_async_remote_copy(
            src_ref=got.at[others], dst_ref=got.at[others], send_sem=piece_send, recv_sem=piece_recv,
            device_id=(li, (vi + 1) % view_count), device_id_type=MESH)

    for k in range(chunks):
        load(k).start()
    coef_copy = pltpu.make_async_copy(coef_hbm, coef_s, coef_sem)
    coef_copy.start()

    barrier = pltpu.get_barrier_semaphore()

    @pl.when(core == 1)
    def _():
        pl.semaphore_signal(barrier, inc=1, device_id=(li - 1, vi), device_id_type=MESH)

    for c in range(chips - 1):
        @pl.when(c < chip)
        def _():
            pl.semaphore_signal(barrier, inc=1, device_id=(2 * c + 1, vi), device_id_type=MESH)

    for turn in range(1, chunks):
        for j in (((vx + turn) % chunks) * per_chunk + vy, vx * per_chunk + (vy + turn) % per_chunk):
            pl.semaphore_signal(barrier, inc=1, device_id=(li, j), device_id_type=MESH)

    term_row = lax.broadcasted_iota(jnp.int32, (3 * ROWS, lanes), 0) % ROWS
    for q in range(ROWS):
        picks[q] = jnp.where(term_row == q, 1.0, 0.0).astype(BF16)

    row = lax.broadcasted_iota(jnp.int32, (ROWS, lanes), 0)
    def sum_up(k):
        load(k).wait()
        acc = jnp.zeros((steps, BLOCK * ROWS), F32)
        for p in range(steps):
            xb = xv[k, p * BLOCK : (p + 1) * BLOCK].reshape(BLOCK * ROWS, lanes)
            pick = jnp.where(row == p, 1.0, 0.0).astype(BF16)[:steps]
            acc = acc + lax.dot_general(pick, xb, (((1,), (1,)), ((), ())), preferred_element_type=F32)
        own_sum[k, 0:steps] = acc[:, : HALF * ROWS]
        own_sum[k, steps:] = acc[:, HALF * ROWS :]

    def meet():
        pl.semaphore_wait(barrier, chunks + per_chunk - 2 + jnp.where(core == 0, 1, 2 * (chips - 1 - chip)))

        for turn in range(1, per_chunk):
            j = vx * per_chunk + (vy + turn) % per_chunk
            pl.semaphore_signal(lines, inc=1, device_id=(li, j), device_id_type=MESH)

    def share():
        @pl.when(core == 0)
        def _():
            for g in range(len(GROUPS)):
                sib_copy(g).start()

    def lower(by):
        if by == 1:
            @pl.when(core == 1)
            def _():
                for g in range(len(GROUPS)):
                    sib_copy(g).wait_recv()
                chip_sum[...] = own_sum[...] + sib_sum[...]

        @pl.when((core == 1) & (chip + by < chips))
        def _():
            for g in range(len(GROUPS)):
                for to_core in range(2):
                    low_copy(g, by, to_core).start()

    view_scale = -LOG2E * 2.0 / view_total
    light_scale = -LOG2E * 2.0 / light_total
    r = lax.broadcasted_iota(jnp.int32, (lanes, lanes), 0)
    c = lax.broadcasted_iota(jnp.int32, (lanes, lanes), 1)
    before = jnp.where(r < c, 1.0, 0.0).astype(BF16)
    def near_side(k):
        def local(b, clear):
            xb = xv[k, pl.ds(b * BLOCK, BLOCK)].reshape(BLOCK * ROWS, lanes)
            depth = jnp.dot(xb, before, preferred_element_type=F32).reshape(BLOCK, ROWS, lanes)
            xb = xb.reshape(BLOCK, ROWS, lanes)
            for v in range(BLOCK):
                x = xb[v].astype(F32)
                beyond = clear * jnp.exp2(view_scale * x)
                a = clear - beyond
                clear = beyond
                alpha[k, b * BLOCK + v] = a
                lit_alpha[k, b * BLOCK + v] = a * jnp.exp2(light_scale * depth[v])
            return clear

        clears[k] = lax.fori_loop(0, steps, local, jnp.ones((ROWS, lanes), F32), unroll=8)

    def arrive(g):
        first, count = GROUPS[g]
        ks = pl.ds(first, count)

        @pl.when(core == 0)
        def _():
            upper[ks] = jnp.zeros((count, ROWS, lanes), F32)

        @pl.when(core == 1)
        def _():
            upper[ks] = sib_sum[ks]

        for c in range(chips - 1):
            @pl.when(c < chip)
            def _():
                low_arrival(g, c).wait_recv()
                upper[ks] += low_sum[c, ks]

        for k in range(first, first + count):
            rest = jnp.exp2(light_scale * upper[k]) * (1.0 / AMBIENT)
            terms = []
            for _ in range(3):
                term = rest.astype(BF16).astype(F32)
                rest = rest - term
                terms.append(term)
            turned = jnp.transpose(jnp.concatenate(terms, axis=0))
            for z in range(2):
                part = [turned[i * ROWS + z * HROWS : i * ROWS + (z + 1) * HROWS] for i in range(HALF)]
                dims[k, z] = jnp.concatenate(part, axis=0).astype(BF16)

    def nearness(k, z, q):
        return jnp.dot(dims[k, z], picks[q], preferred_element_type=F32).reshape(HALF, HROWS, lanes)

    ahead = {}

    def light_up(k, z, then=None):
        zs = slice(z * HROWS, (z + 1) * HROWS)
        sums = [[jnp.zeros((HROWS, lanes), F32) for _ in range(4)] for _ in range(2)]
        for p in range(steps):
            for h in range(2):
                q = p + h * steps
                near = ahead.pop((k, z), None) if q == 0 else None
                near = nearness(k, z, q) if near is None else near
                for i in range(HALF):
                    v = p * BLOCK + h * HALF + i
                    x = xv[k, v].astype(F32)[zs]
                    a = alpha[k, v, zs] + lit_alpha[k, v, zs] * near[i]
                    acc = sums[i % 2]
                    for power in range(4):
                        acc[power] = acc[power] + a
                        if power < 3:
                            a = a * x
        if then is not None:
            ahead[then] = nearness(*then, 0)
        m0, m1, m2, m3 = (even + odd for even, odd in zip(*sums))
        parts = []
        for ch in range(3):
            t = coef_s[ch, 0] * m0 + coef_s[ch, 1] * m1 + coef_s[ch, 2] * m2 + coef_s[ch, 3] * m3
            parts.append(AMBIENT * t)
        parts.append(clears[k, zs])
        if k == 0 and z == 0:
            pl.semaphore_wait(lines, per_chunk - 1)
        half = per_chunk // 2
        for d in range(z * half, (z + 1) * half):
            j = TURN[k] * per_chunk + d
            first = (d - z * half) * rows
            mine = jnp.concatenate([p[first : first + rows] for p in parts], axis=0)
            piece[k, d] = mine
            got[jnp.where(j == vi, vi, view_count)] = mine
        for d in range(z * half, (z + 1) * half):
            j = TURN[k] * per_chunk + d

            @pl.when(j != vi)
            def _():
                piece_copy(k, d, j).start()

    def low_chips():
        meet()
        for by in range(1, chips):
            lower(by)

    for k in range(chunks):
        sum_up(k)
    pl.when(core == 0)(meet)
    share()
    near_side(0)
    near_side(1)
    pl.when((core == 1) & (chip > 0))(low_chips)
    near_side(2)
    pl.when((core == 1) & (chip == 0))(low_chips)
    coef_copy.wait()
    near_side(3)
    arrive(0)
    light_up(0, 0, (0, 1))
    light_up(0, 1)
    arrive(1)
    halves = ((1, 0), (2, 0), (1, 1), (3, 0), (2, 1), (3, 1))
    for half, then in zip(halves, halves[1:] + (None,)):
        light_up(*half, then)

    all_pieces().wait_recv()
    half = lax.broadcasted_iota(jnp.int32, (2 * rows, lanes), 0)
    clear = jnp.ones((2 * rows, lanes), F32)
    total = [jnp.zeros((2 * rows, lanes), F32) for _ in range(2)]
    for i in range(view_count):
        first, second = got[i, : 2 * rows], got[i, 2 * rows :]
        total[0] = total[0] + clear * first
        total[1] = total[1] + clear * second
        clear = clear * jnp.where(half < rows, pltpu.roll(second, rows, 0), second)
    out_ref[0] = total[0][:rows]
    out_ref[1] = total[0][rows:]
    out_ref[2] = total[1][:rows]

    all_pieces().wait_send()

    @pl.when(core == 0)
    def _():
        for g in range(len(GROUPS)):
            sib_copy(g).wait_send()

    for by in range(1, chips):
        @pl.when((core == 1) & (chip + by < chips))
        def _():
            for g in range(len(GROUPS)):
                for to_core in range(2):
                    low_copy(g, by, to_core).wait_send()


def body(density, color_coef):
    cells, planes, lanes = density.shape
    light_count = lax.axis_size("light")
    view_count = lax.axis_size("view")
    chips = light_count // 2
    chunks = planes // ROWS
    rows = planes // view_count
    per_chunk = ROWS // rows
    dma = pltpu.SemaphoreType.DMA
    return pl.pallas_call(
        functools.partial(kernel, lanes * light_count, cells * view_count, light_count, view_count),
        out_shape=pltpu.VMEM((3, rows, lanes), F32),
        in_specs=[pl.BlockSpec(memory_space=pl.ANY), pl.BlockSpec(memory_space=pl.ANY)],
        out_specs=pl.BlockSpec(memory_space=pltpu.VMEM),
        scratch_shapes=[
            pltpu.VMEM((chunks, cells, ROWS, lanes), BF16),
            pltpu.SMEM((3, 4), F32),
            pltpu.VMEM((chunks, ROWS, lanes), F32),
            pltpu.VMEM((chunks, ROWS, lanes), F32),
            pltpu.VMEM((chunks, ROWS, lanes), F32),
            pltpu.VMEM((chips - 1, chunks, ROWS, lanes), F32),
            pltpu.VMEM((chunks, ROWS, lanes), F32),
            pltpu.VMEM((ROWS, 3 * ROWS, lanes), BF16),
            pltpu.VMEM((chunks, 2, lanes // 2, 3 * ROWS), BF16),
            pltpu.VMEM((chunks, cells, ROWS, lanes), F32),
            pltpu.VMEM((chunks, cells, ROWS, lanes), F32),
            pltpu.VMEM((chunks, ROWS, lanes), F32),
            pltpu.VMEM((chunks, per_chunk, 4 * rows, lanes), F32),
            pltpu.VMEM((view_count + 1, 4 * rows, lanes), F32),
            dma((chunks,)),
            dma,
            dma((len(GROUPS),)),
            dma((len(GROUPS),)),
            dma((chips - 1, 2, len(GROUPS))),
            dma((chips - 1, len(GROUPS))),
            dma,
            dma,
            pltpu.SemaphoreType.REGULAR,
        ],
        compiler_params=pltpu.CompilerParams(collective_id=0, has_side_effects=True),
    )(density, color_coef)


def solution(mesh):
    placed = (P("view", None, "light"), P())
    return jax.shard_map(
        body, mesh=mesh, in_specs=placed, out_specs=P(None, "view", "light"), check_vma=False
    )
```

```python
import functools
import math

import jax
import jax.numpy as jnp
from jax import lax
from jax.experimental import pallas as pl
from jax.experimental.pallas import tpu as pltpu
from jax.sharding import PartitionSpec as P

F32 = jnp.float32
BF16 = jnp.bfloat16
LOG2E = math.log2(math.e)
ROWS = 16
BLOCK = 16
HALF = BLOCK // 2
HROWS = ROWS // 2
TURN = (0, 1, 3, 2)
GROUPS = ((0, 1), (1, 3))
AMBIENT = 0.3
MESH = pl.DeviceIdType.MESH


def kernel(
    light_total, view_total, light_count, view_count,
    x_hbm, coef_hbm, out_ref,
    xv, coef_s, own_sum, sib_sum, chip_sum, low_sum, upper, picks, dims, alpha, lit_alpha, clears, piece, got,
    x_sem, coef_sem, sib_send, sib_recv, low_send, low_recv, piece_send, piece_recv, lines,
):
    li = lax.axis_index("light")
    vi = lax.axis_index("view")
    chip, core = li // 2, li % 2
    chips = light_count // 2
    cells, planes, lanes = x_hbm.shape
    chunks = planes // ROWS
    rows = planes // view_count
    per_chunk = ROWS // rows
    steps = cells // BLOCK
    vx, vy = vi // per_chunk, vi % per_chunk

    def load(k):
        z0 = TURN[k] * ROWS
        return pltpu.make_async_copy(x_hbm.at[:, pl.ds(z0, ROWS), :], xv.at[k], x_sem.at[k])

    def sib_copy(g):
        ks = pl.ds(*GROUPS[g])
        return pltpu.make_async_remote_copy(
            src_ref=own_sum.at[ks], dst_ref=sib_sum.at[ks], send_sem=sib_send.at[g], recv_sem=sib_recv.at[g],
            device_id=(chip * 2 + 1, vi), device_id_type=MESH)

    def low_copy(g, by, to_core):
        ks = pl.ds(*GROUPS[g])
        return pltpu.make_async_remote_copy(
            src_ref=chip_sum.at[ks], dst_ref=low_sum.at[chip, ks],
            send_sem=low_send.at[by - 1, to_core, g], recv_sem=low_recv.at[chip, g],
            device_id=((chip + by) * 2 + to_core, vi), device_id_type=MESH)

    def low_arrival(g, c):
        ks = pl.ds(*GROUPS[g])
        return pltpu.make_async_remote_copy(
            src_ref=chip_sum.at[ks], dst_ref=low_sum.at[c, ks],
            send_sem=low_send.at[0, 0, g], recv_sem=low_recv.at[c, g],
            device_id=(c * 2 + 1, vi), device_id_type=MESH)

    def piece_copy(k, d, j):
        return pltpu.make_async_remote_copy(
            src_ref=piece.at[k, d], dst_ref=got.at[vi], send_sem=piece_send, recv_sem=piece_recv,
            device_id=(li, j), device_id_type=MESH)

    def all_pieces():
        others = pl.ds(0, view_count - 1)
        return pltpu.make_async_remote_copy(
            src_ref=got.at[others], dst_ref=got.at[others], send_sem=piece_send, recv_sem=piece_recv,
            device_id=(li, (vi + 1) % view_count), device_id_type=MESH)

    for k in range(chunks):
        load(k).start()
    coef_copy = pltpu.make_async_copy(coef_hbm, coef_s, coef_sem)
    coef_copy.start()

    barrier = pltpu.get_barrier_semaphore()

    @pl.when(core == 1)
    def _():
        pl.semaphore_signal(barrier, inc=1, device_id=(li - 1, vi), device_id_type=MESH)

    for c in range(chips - 1):
        @pl.when(c < chip)
        def _():
            pl.semaphore_signal(barrier, inc=1, device_id=(2 * c + 1, vi), device_id_type=MESH)

    for turn in range(1, chunks):
        for j in (((vx + turn) % chunks) * per_chunk + vy, vx * per_chunk + (vy + turn) % per_chunk):
            pl.semaphore_signal(barrier, inc=1, device_id=(li, j), device_id_type=MESH)

    term_row = lax.broadcasted_iota(jnp.int32, (3 * ROWS, lanes), 0) % ROWS
    for q in range(ROWS):
        picks[q] = jnp.where(term_row == q, 1.0, 0.0).astype(BF16)

    row = lax.broadcasted_iota(jnp.int32, (ROWS, lanes), 0)
    def sum_up(k):
        load(k).wait()
        acc = jnp.zeros((steps, BLOCK * ROWS), F32)
        for p in range(steps):
            xb = xv[k, p * BLOCK : (p + 1) * BLOCK].reshape(BLOCK * ROWS, lanes)
            pick = jnp.where(row == p, 1.0, 0.0).astype(BF16)[:steps]
            acc = acc + lax.dot_general(pick, xb, (((1,), (1,)), ((), ())), preferred_element_type=F32)
        own_sum[k, 0:steps] = acc[:, : HALF * ROWS]
        own_sum[k, steps:] = acc[:, HALF * ROWS :]

    def meet():
        pl.semaphore_wait(barrier, chunks + per_chunk - 2 + jnp.where(core == 0, 1, 2 * (chips - 1 - chip)))

        for turn in range(1, per_chunk):
            j = vx * per_chunk + (vy + turn) % per_chunk
            pl.semaphore_signal(lines, inc=1, device_id=(li, j), device_id_type=MESH)

    def share():
        for g in range(len(GROUPS)):
            sib_copy(g).start()

    def lower():
        for g in range(len(GROUPS)):
            sib_copy(g).wait_recv()
        chip_sum[...] = own_sum[...] + sib_sum[...]
        for c in range(chips - 1):
            @pl.when(chip == c)
            def _():
                for g in range(len(GROUPS)):
                    for to_core in range(2):
                        for by in range(1, chips - c):
                            low_copy(g, by, to_core).start()

    view_scale = -LOG2E * 2.0 / view_total
    light_scale = -LOG2E * 2.0 / light_total
    r = lax.broadcasted_iota(jnp.int32, (lanes, lanes), 0)
    c = lax.broadcasted_iota(jnp.int32, (lanes, lanes), 1)
    before = jnp.where(r < c, 1.0, 0.0).astype(BF16)
    def near_side(k):
        def local(b, clear):
            xb = xv[k, pl.ds(b * BLOCK, BLOCK)].reshape(BLOCK * ROWS, lanes)
            depth = jnp.dot(xb, before, preferred_element_type=F32).reshape(BLOCK, ROWS, lanes)
            xb = xb.reshape(BLOCK, ROWS, lanes)
            for v in range(BLOCK):
                x = xb[v].astype(F32)
                beyond = clear * jnp.exp2(view_scale * x)
                a = clear - beyond
                clear = beyond
                alpha[k, b * BLOCK + v] = a
                lit_alpha[k, b * BLOCK + v] = a * jnp.exp2(light_scale * depth[v])
            return clear

        clears[k] = lax.fori_loop(0, steps, local, jnp.ones((ROWS, lanes), F32), unroll=8)

    def arrive(g):
        first, count = GROUPS[g]
        ks = pl.ds(first, count)

        @pl.when(core == 0)
        def _():
            upper[ks] = jnp.zeros((count, ROWS, lanes), F32)

        @pl.when(core == 1)
        def _():
            upper[ks] = sib_sum[ks]

        for c in range(chips - 1):
            @pl.when(c < chip)
            def _():
                low_arrival(g, c).wait_recv()
                upper[ks] += low_sum[c, ks]

        for k in range(first, first + count):
            rest = jnp.exp2(light_scale * upper[k]) * (1.0 / AMBIENT)
            terms = []
            for _ in range(3):
                term = rest.astype(BF16).astype(F32)
                rest = rest - term
                terms.append(term)
            turned = jnp.transpose(jnp.concatenate(terms, axis=0))
            for z in range(2):
                part = [turned[i * ROWS + z * HROWS : i * ROWS + (z + 1) * HROWS] for i in range(HALF)]
                dims[k, z] = jnp.concatenate(part, axis=0).astype(BF16)

    def nearness(k, z, q):
        return jnp.dot(dims[k, z], picks[q], preferred_element_type=F32).reshape(HALF, HROWS, lanes)

    ahead = {}

    def light_up(k, z, then=None):
        zs = slice(z * HROWS, (z + 1) * HROWS)
        sums = [[jnp.zeros((HROWS, lanes), F32) for _ in range(4)] for _ in range(2)]
        for p in range(steps):
            for h in range(2):
                q = p + h * steps
                near = ahead.pop((k, z), None) if q == 0 else None
                near = nearness(k, z, q) if near is None else near
                for i in range(HALF):
                    v = p * BLOCK + h * HALF + i
                    x = xv[k, v].astype(F32)[zs]
                    a = alpha[k, v, zs] + lit_alpha[k, v, zs] * near[i]
                    acc = sums[i % 2]
                    for power in range(4):
                        acc[power] = acc[power] + a
                        if power < 3:
                            a = a * x
        if then is not None:
            ahead[then] = nearness(*then, 0)
        m0, m1, m2, m3 = (even + odd for even, odd in zip(*sums))
        parts = []
        for ch in range(3):
            t = coef_s[ch, 0] * m0 + coef_s[ch, 1] * m1 + coef_s[ch, 2] * m2 + coef_s[ch, 3] * m3
            parts.append(AMBIENT * t)
        parts.append(clears[k, zs])
        if k == 0 and z == 0:
            pl.semaphore_wait(lines, per_chunk - 1)
        half = per_chunk // 2
        for d in range(z * half, (z + 1) * half):
            j = TURN[k] * per_chunk + d
            first = (d - z * half) * rows
            mine = jnp.concatenate([p[first : first + rows] for p in parts], axis=0)
            piece[k, d] = mine
            got[jnp.where(j == vi, vi, view_count)] = mine
        for d in range(z * half, (z + 1) * half):
            j = TURN[k] * per_chunk + d

            @pl.when(j != vi)
            def _():
                piece_copy(k, d, j).start()

    def low_chips():
        meet()
        lower()

    def sibling():
        meet()
        share()

    edge = (vx == 0) | (vy == 0)
    for k in range(chunks):
        sum_up(k)
    pl.when((core == 0) & ~edge)(sibling)
    near_side(0)
    near_side(1)
    pl.when((core == 0) & edge)(sibling)
    pl.when((core == 1) & (chip > 0))(low_chips)
    near_side(2)
    pl.when((core == 1) & (chip == 0))(low_chips)
    coef_copy.wait()
    near_side(3)
    arrive(0)
    light_up(0, 0, (0, 1))
    light_up(0, 1)
    arrive(1)
    halves = ((1, 0), (2, 0), (1, 1), (3, 0), (2, 1), (3, 1))
    for half, then in zip(halves, halves[1:] + (None,)):
        light_up(*half, then)

    all_pieces().wait_recv()
    half = lax.broadcasted_iota(jnp.int32, (2 * rows, lanes), 0)
    clear = jnp.ones((2 * rows, lanes), F32)
    total = [jnp.zeros((2 * rows, lanes), F32) for _ in range(2)]
    for i in range(view_count):
        first, second = got[i, : 2 * rows], got[i, 2 * rows :]
        total[0] = total[0] + clear * first
        total[1] = total[1] + clear * second
        clear = clear * jnp.where(half < rows, pltpu.roll(second, rows, 0), second)
    out_ref[0] = total[0][:rows]
    out_ref[1] = total[0][rows:]
    out_ref[2] = total[1][:rows]

    all_pieces().wait_send()

    @pl.when(core == 0)
    def _():
        for g in range(len(GROUPS)):
            sib_copy(g).wait_send()

    for by in range(1, chips):
        @pl.when((core == 1) & (chip + by < chips))
        def _():
            for g in range(len(GROUPS)):
                for to_core in range(2):
                    low_copy(g, by, to_core).wait_send()


def body(density, color_coef):
    cells, planes, lanes = density.shape
    light_count = lax.axis_size("light")
    view_count = lax.axis_size("view")
    chips = light_count // 2
    chunks = planes // ROWS
    rows = planes // view_count
    per_chunk = ROWS // rows
    dma = pltpu.SemaphoreType.DMA
    return pl.pallas_call(
        functools.partial(kernel, lanes * light_count, cells * view_count, light_count, view_count),
        out_shape=pltpu.VMEM((3, rows, lanes), F32),
        in_specs=[pl.BlockSpec(memory_space=pl.ANY), pl.BlockSpec(memory_space=pl.ANY)],
        out_specs=pl.BlockSpec(memory_space=pltpu.VMEM),
        scratch_shapes=[
            pltpu.VMEM((chunks, cells, ROWS, lanes), BF16),
            pltpu.SMEM((3, 4), F32),
            pltpu.VMEM((chunks, ROWS, lanes), F32),
            pltpu.VMEM((chunks, ROWS, lanes), F32),
            pltpu.VMEM((chunks, ROWS, lanes), F32),
            pltpu.VMEM((chips - 1, chunks, ROWS, lanes), F32),
            pltpu.VMEM((chunks, ROWS, lanes), F32),
            pltpu.VMEM((ROWS, 3 * ROWS, lanes), BF16),
            pltpu.VMEM((chunks, 2, lanes // 2, 3 * ROWS), BF16),
            pltpu.VMEM((chunks, cells, ROWS, lanes), F32),
            pltpu.VMEM((chunks, cells, ROWS, lanes), F32),
            pltpu.VMEM((chunks, ROWS, lanes), F32),
            pltpu.VMEM((chunks, per_chunk, 4 * rows, lanes), F32),
            pltpu.VMEM((view_count + 1, 4 * rows, lanes), F32),
            dma((chunks,)),
            dma,
            dma((len(GROUPS),)),
            dma((len(GROUPS),)),
            dma((chips - 1, 2, len(GROUPS))),
            dma((chips - 1, len(GROUPS))),
            dma,
            dma,
            pltpu.SemaphoreType.REGULAR,
        ],
        compiler_params=pltpu.CompilerParams(collective_id=0, has_side_effects=True),
    )(density, color_coef)


def solution(mesh):
    placed = (P("view", None, "light"), P())
    return jax.shard_map(
        body, mesh=mesh, in_specs=placed, out_specs=P(None, "view", "light"), check_vma=False
    )
```

```python
import functools
import math

import jax
import jax.numpy as jnp
from jax import lax
from jax.experimental import pallas as pl
from jax.experimental.pallas import tpu as pltpu
from jax.sharding import PartitionSpec as P

F32 = jnp.float32
BF16 = jnp.bfloat16
LOG2E = math.log2(math.e)
ROWS = 16
BLOCK = 16
HALF = BLOCK // 2
HROWS = ROWS // 2
TURN = (0, 1, 3, 2)
GROUPS = ((0, 1), (1, 3))
AMBIENT = 0.3
MESH = pl.DeviceIdType.MESH


def kernel(
    light_total, view_total, light_count, view_count,
    x_hbm, coef_hbm, out_ref,
    xv, coef_s, own_sum, sib_sum, chip_sum, low_sum, upper, picks, dims, alpha, lit_alpha, clears, piece, got,
    x_sem, coef_sem, sib_send, sib_recv, low_send, low_recv, piece_send, piece_recv, lines,
):
    li = lax.axis_index("light")
    vi = lax.axis_index("view")
    chip, core = li // 2, li % 2
    chips = light_count // 2
    cells, planes, lanes = x_hbm.shape
    chunks = planes // ROWS
    rows = planes // view_count
    per_chunk = ROWS // rows
    steps = cells // BLOCK
    vx, vy = vi // per_chunk, vi % per_chunk

    def load(k):
        z0 = TURN[k] * ROWS
        return pltpu.make_async_copy(x_hbm.at[:, pl.ds(z0, ROWS), :], xv.at[k], x_sem.at[k])

    def sib_copy(g):
        ks = pl.ds(*GROUPS[g])
        return pltpu.make_async_remote_copy(
            src_ref=own_sum.at[ks], dst_ref=sib_sum.at[ks], send_sem=sib_send.at[g], recv_sem=sib_recv.at[g],
            device_id=(chip * 2 + 1, vi), device_id_type=MESH)

    def low_copy(g, by, to_core):
        ks = pl.ds(*GROUPS[g])
        return pltpu.make_async_remote_copy(
            src_ref=chip_sum.at[ks], dst_ref=low_sum.at[chip, ks],
            send_sem=low_send.at[by - 1, to_core, g], recv_sem=low_recv.at[chip, g],
            device_id=((chip + by) * 2 + to_core, vi), device_id_type=MESH)

    def low_arrival(g, c):
        ks = pl.ds(*GROUPS[g])
        return pltpu.make_async_remote_copy(
            src_ref=chip_sum.at[ks], dst_ref=low_sum.at[c, ks],
            send_sem=low_send.at[0, 0, g], recv_sem=low_recv.at[c, g],
            device_id=(c * 2 + 1, vi), device_id_type=MESH)

    def piece_copy(k, d, j):
        return pltpu.make_async_remote_copy(
            src_ref=piece.at[k, d], dst_ref=got.at[vi], send_sem=piece_send, recv_sem=piece_recv,
            device_id=(li, j), device_id_type=MESH)

    def all_pieces():
        others = pl.ds(0, view_count - 1)
        return pltpu.make_async_remote_copy(
            src_ref=got.at[others], dst_ref=got.at[others], send_sem=piece_send, recv_sem=piece_recv,
            device_id=(li, (vi + 1) % view_count), device_id_type=MESH)

    for k in range(chunks):
        load(k).start()
    coef_copy = pltpu.make_async_copy(coef_hbm, coef_s, coef_sem)
    coef_copy.start()

    barrier = pltpu.get_barrier_semaphore()

    @pl.when(core == 1)
    def _():
        pl.semaphore_signal(barrier, inc=1, device_id=(li - 1, vi), device_id_type=MESH)

    for c in range(chips - 1):
        @pl.when(c < chip)
        def _():
            pl.semaphore_signal(barrier, inc=1, device_id=(2 * c + 1, vi), device_id_type=MESH)

    for turn in range(1, chunks):
        for j in (((vx + turn) % chunks) * per_chunk + vy, vx * per_chunk + (vy + turn) % per_chunk):
            pl.semaphore_signal(barrier, inc=1, device_id=(li, j), device_id_type=MESH)

    term_row = lax.broadcasted_iota(jnp.int32, (3 * ROWS, lanes), 0) % ROWS
    for q in range(ROWS):
        picks[q] = jnp.where(term_row == q, 1.0, 0.0).astype(BF16)

    row = lax.broadcasted_iota(jnp.int32, (ROWS, lanes), 0)
    def sum_up(k):
        load(k).wait()
        acc = jnp.zeros((steps, BLOCK * ROWS), F32)
        for p in range(steps):
            xb = xv[k, p * BLOCK : (p + 1) * BLOCK].reshape(BLOCK * ROWS, lanes)
            pick = jnp.where(row == p, 1.0, 0.0).astype(BF16)[:steps]
            acc = acc + lax.dot_general(pick, xb, (((1,), (1,)), ((), ())), preferred_element_type=F32)
        own_sum[k, 0:steps] = acc[:, : HALF * ROWS]
        own_sum[k, steps:] = acc[:, HALF * ROWS :]

    def meet():
        pl.semaphore_wait(barrier, chunks + per_chunk - 2 + jnp.where(core == 0, 1, 2 * (chips - 1 - chip)))

        for turn in range(1, per_chunk):
            j = vx * per_chunk + (vy + turn) % per_chunk
            pl.semaphore_signal(lines, inc=1, device_id=(li, j), device_id_type=MESH)

    def share():
        for g in range(len(GROUPS)):
            sib_copy(g).start()

    def lower():
        for g in range(len(GROUPS)):
            sib_copy(g).wait_recv()
        chip_sum[...] = own_sum[...] + sib_sum[...]
        for c in range(chips - 1):
            @pl.when(chip == c)
            def _():
                for g in range(len(GROUPS)):
                    for to_core in range(2):
                        for by in range(1, chips - c):
                            low_copy(g, by, to_core).start()

    view_scale = -LOG2E * 2.0 / view_total
    light_scale = -LOG2E * 2.0 / light_total
    r = lax.broadcasted_iota(jnp.int32, (lanes, lanes), 0)
    c = lax.broadcasted_iota(jnp.int32, (lanes, lanes), 1)
    before = jnp.where(r < c, 1.0, 0.0).astype(BF16)
    def near_side(k):
        def local(b, clear):
            xb = xv[k, pl.ds(b * BLOCK, BLOCK)].reshape(BLOCK * ROWS, lanes)
            depth = jnp.dot(xb, before, preferred_element_type=F32).reshape(BLOCK, ROWS, lanes)
            xb = xb.reshape(BLOCK, ROWS, lanes)
            for v in range(BLOCK):
                x = xb[v].astype(F32)
                beyond = clear * jnp.exp2(view_scale * x)
                a = clear - beyond
                clear = beyond
                alpha[k, b * BLOCK + v] = a
                lit_alpha[k, b * BLOCK + v] = a * jnp.exp2(light_scale * depth[v])
            return clear

        clears[k] = lax.fori_loop(0, steps, local, jnp.ones((ROWS, lanes), F32), unroll=8)

    def arrive(g):
        first, count = GROUPS[g]
        ks = pl.ds(first, count)

        @pl.when(core == 0)
        def _():
            upper[ks] = jnp.zeros((count, ROWS, lanes), F32)

        @pl.when(core == 1)
        def _():
            upper[ks] = sib_sum[ks]

        for c in range(chips - 1):
            @pl.when(c < chip)
            def _():
                low_arrival(g, c).wait_recv()
                upper[ks] += low_sum[c, ks]

        for k in range(first, first + count):
            rest = jnp.exp2(light_scale * upper[k]) * (1.0 / AMBIENT)
            terms = []
            for _ in range(3):
                term = rest.astype(BF16).astype(F32)
                rest = rest - term
                terms.append(term)
            turned = jnp.transpose(jnp.concatenate(terms, axis=0))
            for z in range(2):
                part = [turned[i * ROWS + z * HROWS : i * ROWS + (z + 1) * HROWS] for i in range(HALF)]
                dims[k, z] = jnp.concatenate(part, axis=0).astype(BF16)

    def nearness(k, z, q):
        return jnp.dot(dims[k, z], picks[q], preferred_element_type=F32).reshape(HALF, HROWS, lanes)

    ahead = {}

    def light_up(k, z, then=None):
        zs = slice(z * HROWS, (z + 1) * HROWS)
        sums = [[jnp.zeros((HROWS, lanes), F32) for _ in range(4)] for _ in range(2)]
        for p in range(steps):
            for h in range(2):
                q = p + h * steps
                near = ahead.pop((k, z), None) if q == 0 else None
                near = nearness(k, z, q) if near is None else near
                for i in range(HALF):
                    v = p * BLOCK + h * HALF + i
                    x = xv[k, v].astype(F32)[zs]
                    a = alpha[k, v, zs] + lit_alpha[k, v, zs] * near[i]
                    acc = sums[i % 2]
                    for power in range(4):
                        acc[power] = acc[power] + a
                        if power < 3:
                            a = a * x
        if then is not None:
            ahead[then] = nearness(*then, 0)
        m0, m1, m2, m3 = (even + odd for even, odd in zip(*sums))
        parts = []
        for ch in range(3):
            t = coef_s[ch, 0] * m0 + coef_s[ch, 1] * m1 + coef_s[ch, 2] * m2 + coef_s[ch, 3] * m3
            parts.append(AMBIENT * t)
        parts.append(clears[k, zs])
        if k == 0 and z == 0:
            pl.semaphore_wait(lines, per_chunk - 1)
        half = per_chunk // 2
        for d in range(z * half, (z + 1) * half):
            j = TURN[k] * per_chunk + d
            first = (d - z * half) * rows
            mine = jnp.concatenate([p[first : first + rows] for p in parts], axis=0)
            piece[k, d] = mine
            got[jnp.where(j == vi, vi, view_count)] = mine
        for d in range(z * half, (z + 1) * half):
            j = TURN[k] * per_chunk + d

            @pl.when(j != vi)
            def _():
                piece_copy(k, d, j).start()

    def low_chips():
        meet()
        lower()

    def sibling():
        meet()
        share()

    edge = (vx == 0) | (vy == 0)
    for k in range(chunks):
        sum_up(k)
    pl.when((core == 0) & ~edge)(sibling)
    near_side(0)
    near_side(1)
    pl.when((core == 0) & edge)(sibling)
    pl.when((core == 1) & (chip > 0))(low_chips)
    near_side(2)
    pl.when((core == 1) & (chip == 0))(low_chips)
    coef_copy.wait()
    near_side(3)
    arrive(0)
    light_up(0, 0)
    arrive(1)
    halves = ((1, 0), (2, 0), (0, 1), (3, 0), (1, 1), (2, 1), (3, 1))
    for half, then in zip(halves, halves[1:] + (None,)):
        light_up(*half, then)

    all_pieces().wait_recv()
    half = lax.broadcasted_iota(jnp.int32, (2 * rows, lanes), 0)
    clear = jnp.ones((2 * rows, lanes), F32)
    total = [jnp.zeros((2 * rows, lanes), F32) for _ in range(2)]
    for i in range(view_count):
        first, second = got[i, : 2 * rows], got[i, 2 * rows :]
        total[0] = total[0] + clear * first
        total[1] = total[1] + clear * second
        clear = clear * jnp.where(half < rows, pltpu.roll(second, rows, 0), second)
    out_ref[0] = total[0][:rows]
    out_ref[1] = total[0][rows:]
    out_ref[2] = total[1][:rows]

    all_pieces().wait_send()

    @pl.when(core == 0)
    def _():
        for g in range(len(GROUPS)):
            sib_copy(g).wait_send()

    for by in range(1, chips):
        @pl.when((core == 1) & (chip + by < chips))
        def _():
            for g in range(len(GROUPS)):
                for to_core in range(2):
                    low_copy(g, by, to_core).wait_send()


def body(density, color_coef):
    cells, planes, lanes = density.shape
    light_count = lax.axis_size("light")
    view_count = lax.axis_size("view")
    chips = light_count // 2
    chunks = planes // ROWS
    rows = planes // view_count
    per_chunk = ROWS // rows
    dma = pltpu.SemaphoreType.DMA
    return pl.pallas_call(
        functools.partial(kernel, lanes * light_count, cells * view_count, light_count, view_count),
        out_shape=pltpu.VMEM((3, rows, lanes), F32),
        in_specs=[pl.BlockSpec(memory_space=pl.ANY), pl.BlockSpec(memory_space=pl.ANY)],
        out_specs=pl.BlockSpec(memory_space=pltpu.VMEM),
        scratch_shapes=[
            pltpu.VMEM((chunks, cells, ROWS, lanes), BF16),
            pltpu.SMEM((3, 4), F32),
            pltpu.VMEM((chunks, ROWS, lanes), F32),
            pltpu.VMEM((chunks, ROWS, lanes), F32),
            pltpu.VMEM((chunks, ROWS, lanes), F32),
            pltpu.VMEM((chips - 1, chunks, ROWS, lanes), F32),
            pltpu.VMEM((chunks, ROWS, lanes), F32),
            pltpu.VMEM((ROWS, 3 * ROWS, lanes), BF16),
            pltpu.VMEM((chunks, 2, lanes // 2, 3 * ROWS), BF16),
            pltpu.VMEM((chunks, cells, ROWS, lanes), F32),
            pltpu.VMEM((chunks, cells, ROWS, lanes), F32),
            pltpu.VMEM((chunks, ROWS, lanes), F32),
            pltpu.VMEM((chunks, per_chunk, 4 * rows, lanes), F32),
            pltpu.VMEM((view_count + 1, 4 * rows, lanes), F32),
            dma((chunks,)),
            dma,
            dma((len(GROUPS),)),
            dma((len(GROUPS),)),
            dma((chips - 1, 2, len(GROUPS))),
            dma((chips - 1, len(GROUPS))),
            dma,
            dma,
            pltpu.SemaphoreType.REGULAR,
        ],
        compiler_params=pltpu.CompilerParams(collective_id=0, has_side_effects=True),
    )(density, color_coef)


def solution(mesh):
    placed = (P("view", None, "light"), P())
    return jax.shard_map(
        body, mesh=mesh, in_specs=placed, out_specs=P(None, "view", "light"), check_vma=False
    )
```

```python
import functools
import math

import jax
import jax.numpy as jnp
from jax import lax
from jax.experimental import pallas as pl
from jax.experimental.pallas import tpu as pltpu
from jax.sharding import PartitionSpec as P

F32 = jnp.float32
BF16 = jnp.bfloat16
LOG2E = math.log2(math.e)
ROWS = 16
BLOCK = 16
HALF = BLOCK // 2
HROWS = ROWS // 2
TURN = (0, 1, 3, 2)
GROUPS = ((0, 1), (1, 3))
AMBIENT = 0.3
MESH = pl.DeviceIdType.MESH


def kernel(
    light_total, view_total, light_count, view_count,
    x_hbm, coef_hbm, out_ref,
    xv, coef_s, own_sum, sib_sum, chip_sum, low_sum, upper, picks, dims, alpha, lit_alpha, clears, piece, got,
    x_sem, coef_sem, sib_send, sib_recv, low_send, low_recv, piece_send, piece_recv, lines,
):
    li = lax.axis_index("light")
    vi = lax.axis_index("view")
    chip, core = li // 2, li % 2
    chips = light_count // 2
    cells, planes, lanes = x_hbm.shape
    chunks = planes // ROWS
    rows = planes // view_count
    per_chunk = ROWS // rows
    steps = cells // BLOCK
    vx, vy = vi // per_chunk, vi % per_chunk

    def load(k):
        z0 = TURN[k] * ROWS
        return pltpu.make_async_copy(x_hbm.at[:, pl.ds(z0, ROWS), :], xv.at[k], x_sem.at[k])

    def sib_copy(g):
        ks = pl.ds(*GROUPS[g])
        return pltpu.make_async_remote_copy(
            src_ref=own_sum.at[ks], dst_ref=sib_sum.at[ks], send_sem=sib_send.at[g], recv_sem=sib_recv.at[g],
            device_id=(chip * 2 + 1, vi), device_id_type=MESH)

    def low_copy(g, by, to_core):
        ks = pl.ds(*GROUPS[g])
        return pltpu.make_async_remote_copy(
            src_ref=chip_sum.at[ks], dst_ref=low_sum.at[chip, ks],
            send_sem=low_send.at[by - 1, to_core, g], recv_sem=low_recv.at[chip, g],
            device_id=((chip + by) * 2 + to_core, vi), device_id_type=MESH)

    def low_arrival(g, c):
        ks = pl.ds(*GROUPS[g])
        return pltpu.make_async_remote_copy(
            src_ref=chip_sum.at[ks], dst_ref=low_sum.at[c, ks],
            send_sem=low_send.at[0, 0, g], recv_sem=low_recv.at[c, g],
            device_id=(c * 2 + 1, vi), device_id_type=MESH)

    def piece_copy(k, d, j):
        return pltpu.make_async_remote_copy(
            src_ref=piece.at[k, d], dst_ref=got.at[vi], send_sem=piece_send, recv_sem=piece_recv,
            device_id=(li, j), device_id_type=MESH)

    def all_pieces():
        others = pl.ds(0, view_count - 1)
        return pltpu.make_async_remote_copy(
            src_ref=got.at[others], dst_ref=got.at[others], send_sem=piece_send, recv_sem=piece_recv,
            device_id=(li, (vi + 1) % view_count), device_id_type=MESH)

    for k in range(chunks):
        load(k).start()
    coef_copy = pltpu.make_async_copy(coef_hbm, coef_s, coef_sem)
    coef_copy.start()

    barrier = pltpu.get_barrier_semaphore()

    @pl.when(core == 1)
    def _():
        pl.semaphore_signal(barrier, inc=1, device_id=(li - 1, vi), device_id_type=MESH)

    for c in range(chips - 1):
        @pl.when(c < chip)
        def _():
            pl.semaphore_signal(barrier, inc=1, device_id=(2 * c + 1, vi), device_id_type=MESH)

    for turn in range(1, chunks):
        for j in (((vx + turn) % chunks) * per_chunk + vy, vx * per_chunk + (vy + turn) % per_chunk):
            pl.semaphore_signal(barrier, inc=1, device_id=(li, j), device_id_type=MESH)

    term_row = lax.broadcasted_iota(jnp.int32, (3 * ROWS, lanes), 0) % ROWS
    for q in range(ROWS):
        picks[q] = jnp.where(term_row == q, 1.0, 0.0).astype(BF16)

    row = lax.broadcasted_iota(jnp.int32, (ROWS, lanes), 0)
    def sum_up(k):
        load(k).wait()
        acc = jnp.zeros((steps, BLOCK * ROWS), F32)
        for p in range(steps):
            xb = xv[k, p * BLOCK : (p + 1) * BLOCK].reshape(BLOCK * ROWS, lanes)
            pick = jnp.where(row == p, 1.0, 0.0).astype(BF16)[:steps]
            acc = acc + lax.dot_general(pick, xb, (((1,), (1,)), ((), ())), preferred_element_type=F32)
        own_sum[k, 0:steps] = acc[:, : HALF * ROWS]
        own_sum[k, steps:] = acc[:, HALF * ROWS :]

    def meet():
        pl.semaphore_wait(barrier, chunks + per_chunk - 2 + jnp.where(core == 0, 1, 2 * (chips - 1 - chip)))

        for turn in range(1, per_chunk):
            j = vx * per_chunk + (vy + turn) % per_chunk
            pl.semaphore_signal(lines, inc=1, device_id=(li, j), device_id_type=MESH)

    def share():
        for g in range(len(GROUPS)):
            sib_copy(g).start()

    def lower():
        for g in range(len(GROUPS)):
            sib_copy(g).wait_recv()
        chip_sum[...] = own_sum[...] + sib_sum[...]
        for c in range(chips - 1):
            @pl.when(chip == c)
            def _():
                for g in range(len(GROUPS)):
                    for to_core in range(2):
                        for by in range(1, chips - c):
                            low_copy(g, by, to_core).start()

    view_scale = -LOG2E * 2.0 / view_total
    light_scale = -LOG2E * 2.0 / light_total
    r = lax.broadcasted_iota(jnp.int32, (lanes, lanes), 0)
    c = lax.broadcasted_iota(jnp.int32, (lanes, lanes), 1)
    before = jnp.where(r < c, 1.0, 0.0).astype(BF16)
    def near_side(k):
        def local(b, clear):
            xb = xv[k, pl.ds(b * BLOCK, BLOCK)].reshape(BLOCK * ROWS, lanes)
            depth = jnp.dot(xb, before, preferred_element_type=F32).reshape(BLOCK, ROWS, lanes)
            xb = xb.reshape(BLOCK, ROWS, lanes)
            for v in range(BLOCK):
                x = xb[v].astype(F32)
                beyond = clear * jnp.exp2(view_scale * x)
                a = clear - beyond
                clear = beyond
                alpha[k, b * BLOCK + v] = a
                lit_alpha[k, b * BLOCK + v] = a * jnp.exp2(light_scale * depth[v])
            return clear

        clears[k] = lax.fori_loop(0, steps, local, jnp.ones((ROWS, lanes), F32), unroll=8)

    def arrive(g):
        first, count = GROUPS[g]
        ks = pl.ds(first, count)

        @pl.when(core == 0)
        def _():
            upper[ks] = jnp.zeros((count, ROWS, lanes), F32)

        @pl.when(core == 1)
        def _():
            upper[ks] = sib_sum[ks]

        for c in range(chips - 1):
            @pl.when(c < chip)
            def _():
                low_arrival(g, c).wait_recv()
                upper[ks] += low_sum[c, ks]

        for k in range(first, first + count):
            rest = jnp.exp2(light_scale * upper[k]) * (1.0 / AMBIENT)
            terms = []
            for _ in range(3):
                term = rest.astype(BF16).astype(F32)
                rest = rest - term
                terms.append(term)
            turned = jnp.transpose(jnp.concatenate(terms, axis=0))
            for z in range(2):
                part = [turned[i * ROWS + z * HROWS : i * ROWS + (z + 1) * HROWS] for i in range(HALF)]
                dims[k, z] = jnp.concatenate(part, axis=0).astype(BF16)

    def nearness(k, z, q):
        return jnp.dot(dims[k, z], picks[q], preferred_element_type=F32).reshape(HALF, HROWS, lanes)

    ahead = {}

    def light_up(k, z, then=None):
        zs = slice(z * HROWS, (z + 1) * HROWS)
        sums = [[jnp.zeros((HROWS, lanes), F32) for _ in range(4)] for _ in range(2)]
        for p in range(steps):
            for h in range(2):
                q = p + h * steps
                near = ahead.pop((k, z), None) if q == 0 else None
                near = nearness(k, z, q) if near is None else near
                for i in range(HALF):
                    v = p * BLOCK + h * HALF + i
                    x = xv[k, v].astype(F32)[zs]
                    a = alpha[k, v, zs] + lit_alpha[k, v, zs] * near[i]
                    acc = sums[i % 2]
                    for power in range(4):
                        acc[power] = acc[power] + a
                        if power < 3:
                            a = a * x
        if then is not None:
            ahead[then] = nearness(*then, 0)
        m0, m1, m2, m3 = (even + odd for even, odd in zip(*sums))
        parts = []
        for ch in range(3):
            t = coef_s[ch, 0] * m0 + coef_s[ch, 1] * m1 + coef_s[ch, 2] * m2 + coef_s[ch, 3] * m3
            parts.append(AMBIENT * t)
        parts.append(clears[k, zs])
        if k == 0 and z == 0:
            pl.semaphore_wait(lines, per_chunk - 1)
        half = per_chunk // 2
        for d in range(z * half, (z + 1) * half):
            j = TURN[k] * per_chunk + d
            first = (d - z * half) * rows
            mine = jnp.concatenate([p[first : first + rows] for p in parts], axis=0)
            piece[k, d] = mine
            got[jnp.where(j == vi, vi, view_count)] = mine
        for d in range(z * half, (z + 1) * half):
            j = TURN[k] * per_chunk + d

            @pl.when(j != vi)
            def _():
                piece_copy(k, d, j).start()

    def low_chips():
        meet()
        lower()

    def sibling():
        meet()
        share()

    edge = (vx == 0) | (vy == 0)
    for k in range(chunks):
        sum_up(k)
    pl.when((core == 0) & ~edge)(sibling)
    near_side(0)
    near_side(1)
    pl.when((core == 0) & edge)(sibling)
    pl.when((core == 1) & (chip > 0))(low_chips)
    near_side(2)
    pl.when((core == 1) & (chip == 0))(low_chips)
    coef_copy.wait()
    pl.when(chip > 0)(functools.partial(near_side, 3))
    arrive(0)
    light_up(0, 0)
    pl.when(chip == 0)(functools.partial(near_side, 3))
    arrive(1)
    halves = ((1, 0), (2, 0), (0, 1), (3, 0), (1, 1), (2, 1), (3, 1))
    for half, then in zip(halves, halves[1:] + (None,)):
        light_up(*half, then)

    all_pieces().wait_recv()
    half = lax.broadcasted_iota(jnp.int32, (2 * rows, lanes), 0)
    clear = jnp.ones((2 * rows, lanes), F32)
    total = [jnp.zeros((2 * rows, lanes), F32) for _ in range(2)]
    for i in range(view_count):
        first, second = got[i, : 2 * rows], got[i, 2 * rows :]
        total[0] = total[0] + clear * first
        total[1] = total[1] + clear * second
        clear = clear * jnp.where(half < rows, pltpu.roll(second, rows, 0), second)
    out_ref[0] = total[0][:rows]
    out_ref[1] = total[0][rows:]
    out_ref[2] = total[1][:rows]

    all_pieces().wait_send()

    @pl.when(core == 0)
    def _():
        for g in range(len(GROUPS)):
            sib_copy(g).wait_send()

    for by in range(1, chips):
        @pl.when((core == 1) & (chip + by < chips))
        def _():
            for g in range(len(GROUPS)):
                for to_core in range(2):
                    low_copy(g, by, to_core).wait_send()


def body(density, color_coef):
    cells, planes, lanes = density.shape
    light_count = lax.axis_size("light")
    view_count = lax.axis_size("view")
    chips = light_count // 2
    chunks = planes // ROWS
    rows = planes // view_count
    per_chunk = ROWS // rows
    dma = pltpu.SemaphoreType.DMA
    return pl.pallas_call(
        functools.partial(kernel, lanes * light_count, cells * view_count, light_count, view_count),
        out_shape=pltpu.VMEM((3, rows, lanes), F32),
        in_specs=[pl.BlockSpec(memory_space=pl.ANY), pl.BlockSpec(memory_space=pl.ANY)],
        out_specs=pl.BlockSpec(memory_space=pltpu.VMEM),
        scratch_shapes=[
            pltpu.VMEM((chunks, cells, ROWS, lanes), BF16),
            pltpu.SMEM((3, 4), F32),
            pltpu.VMEM((chunks, ROWS, lanes), F32),
            pltpu.VMEM((chunks, ROWS, lanes), F32),
            pltpu.VMEM((chunks, ROWS, lanes), F32),
            pltpu.VMEM((chips - 1, chunks, ROWS, lanes), F32),
            pltpu.VMEM((chunks, ROWS, lanes), F32),
            pltpu.VMEM((ROWS, 3 * ROWS, lanes), BF16),
            pltpu.VMEM((chunks, 2, lanes // 2, 3 * ROWS), BF16),
            pltpu.VMEM((chunks, cells, ROWS, lanes), F32),
            pltpu.VMEM((chunks, cells, ROWS, lanes), F32),
            pltpu.VMEM((chunks, ROWS, lanes), F32),
            pltpu.VMEM((chunks, per_chunk, 4 * rows, lanes), F32),
            pltpu.VMEM((view_count + 1, 4 * rows, lanes), F32),
            dma((chunks,)),
            dma,
            dma((len(GROUPS),)),
            dma((len(GROUPS),)),
            dma((chips - 1, 2, len(GROUPS))),
            dma((chips - 1, len(GROUPS))),
            dma,
            dma,
            pltpu.SemaphoreType.REGULAR,
        ],
        compiler_params=pltpu.CompilerParams(collective_id=0, has_side_effects=True),
    )(density, color_coef)


def solution(mesh):
    placed = (P("view", None, "light"), P())
    return jax.shard_map(
        body, mesh=mesh, in_specs=placed, out_specs=P(None, "view", "light"), check_vma=False
    )
```
